32 devices in a mesh: ctx: 8 (over z, x), tp: 4 (over y, core).
Axes of the slice: x: 2, y: 2, z: 4, core: 2. Of those that a mesh axis runs over, the one named last changes fastest.
Arguments:
- lin_q: bfloat16 [2048, 4096], P('ctx', 'tp'), may hold values from -6 to 6
- lin_k: bfloat16 [2048, 4096], P('ctx', 'tp'), may hold values from -6 to 6
- lin_v: bfloat16 [2048, 4096], P('ctx', 'tp'), may hold values from -20 to 20
- att_q: bfloat16 [2048, 4096], P('ctx', 'tp'), may hold values from -150 to 150
- att_k: bfloat16 [2048, 1024], P('ctx', 'tp'), may hold values from -7 to 7
- att_v: bfloat16 [2048, 1024], P('ctx', 'tp'), may hold values from -20 to 20
- block_lists: int32 [16, 4], P('ctx'), may hold values from -1 to 15, as said below
- gain_lin: bfloat16 [4096], P('tp'), may hold values from 0.25 to 1.75
- gain_att: bfloat16 [4096], P('tp'), may hold values from 0.25 to 1.75
Outputs:
- mixed: bfloat16 [2048, 4096], P('ctx', 'tp')
The draws below stay inside these ranges and needn't reach their ends.
Inputs may be any that keep to these rules, and one draw needn't show every extreme that they name: `block_lists`: row b: entry 0 is b; every other entry is either -1 (unused) or a block in b - 4 to b - 1, with no block twice; some row has all 4 entries in use.
All inputs are finite; a program needn't handle non-finite values.
Results may differ from the reference program's by a relative error of at most 0.0049.
Values may be sent and summed in bfloat16 or wider, within the bound.
A program may use at most 192 MiB of HBM per device.

```python
import jax
import jax.numpy as jnp
from jax import lax

HEADS = 32
KV_HEADS = 8
HD = 128
BLK = 128
SPAN = 5
LIST = 4
SEQ = 2048
NBLK = 16


def attention_pair(key):
    split_keys = jax.random.split(jax.random.fold_in(key, 7), 2)
    keys_all = jnp.clip(jax.random.normal(split_keys[1], (SEQ, KV_HEADS, HD), jnp.float32), -6.0, 6.0)
    queries = jnp.clip(jax.random.normal(split_keys[0], (SEQ, HEADS, HD), jnp.float32), -6.0, 6.0)
    return (queries.reshape(SEQ, HEADS * HD), keys_all.reshape(SEQ, KV_HEADS * HD))


def rising_values(key, heads):
    split_keys = jax.random.split(jax.random.fold_in(key, 3), 1)
    values = jnp.clip(jax.random.normal(split_keys[0], (SEQ, heads, HD), jnp.float32), -6.0, 6.0)
    rising = 3.0 ** (jnp.arange(heads, dtype=jnp.float32) / (heads - 1))
    return (values * rising[None, :, None]).reshape(SEQ, heads * HD).astype(jnp.bfloat16)


def draw_att_q(key, part):
    return attention_pair(key)[0].astype(jnp.bfloat16)


def draw_att_k(key, part):
    return attention_pair(key)[1].astype(jnp.bfloat16)


def draw_lin_v(key, part):
    return rising_values(jax.random.fold_in(key, 21), HEADS)


def draw_att_v(key, part):
    return rising_values(jax.random.fold_in(key, 22), KV_HEADS)


def draw_block_lists(key, part):
    split_keys = jax.random.split(jax.random.fold_in(key, 5), 2)
    block = jnp.arange(NBLK, dtype=jnp.int32)[:, None]
    offsets = jnp.arange(1, SPAN, dtype=jnp.int32)[None, :]
    random_part = jax.random.randint(split_keys[0], (NBLK, SPAN - 1), 0, 65536, jnp.int32)
    ranking = random_part * SPAN + offsets
    valid = block - offsets >= 0
    ranking = jnp.where(valid, ranking, -1 - offsets)
    chosen_rank, chosen_index = jax.lax.top_k(ranking, LIST - 1)
    chosen = block - (chosen_index.astype(jnp.int32) + 1)
    counts = jax.random.randint(split_keys[1], (NBLK, 1), 1, LIST + 1, jnp.int32)
    counts = jnp.where(block == NBLK - 1, LIST, counts)
    slots = jnp.arange(1, LIST, dtype=jnp.int32)[None, :]
    in_use = (slots < counts) & (chosen >= 0)
    others = jnp.where(in_use, chosen, -1)
    return jnp.concatenate([block, others], axis=1).astype(jnp.int32)


def steps_of(stream_key, dims, shards, smallest, top_value):
    gain, own = 1.0, jax.random.fold_in(stream_key, 6)
    for dim, shards_of in shards:
        heights = jnp.exp(jax.random.uniform(jax.random.fold_in(own, dim), (shards_of,), jnp.float32, smallest / len(shards), top_value / len(shards)))
        gain = gain * jnp.repeat(heights, dims[dim] // shards_of).reshape([-1 if axis == dim else 1 for axis in range(len(dims))])
    return gain


def normal_values(rng, dims, width, reach, cuts=(), kind=jnp.bfloat16):
    values = jax.random.normal(rng, dims, jnp.float32) * width
    if len(cuts) > 0:
        values = steps_of(rng, dims, cuts, -0.22, 0.18) * values
    return jnp.clip(values, min=-reach, max=reach).astype(kind)


def setup_inputs(seed: int = 0) -> dict:
    key_list = jax.random.split(jax.random.key(seed), 10)
    lin_q = normal_values(key_list[0], (SEQ, HEADS * HD), 1.0, 6.0, ((0, 8), (1, 4)))
    lin_k = normal_values(key_list[1], (SEQ, HEADS * HD), 1.0, 6.0, ((0, 8), (1, 4)))
    lin_v = draw_lin_v(jax.random.fold_in(key_list[9], 71), 0)
    att_q = draw_att_q(jax.random.fold_in(key_list[9], 71), 0)
    att_k = draw_att_k(jax.random.fold_in(key_list[9], 71), 0)
    att_v = draw_att_v(jax.random.fold_in(key_list[9], 71), 0)
    block_lists = draw_block_lists(jax.random.fold_in(key_list[9], 71), 0)
    gain_lin = jnp.clip(1.0 + 0.15 * jax.random.normal(key_list[7], (HEADS * HD,), jnp.float32), 0.25, 1.75).astype(jnp.bfloat16)
    gain_att = jnp.clip(1.0 + 0.15 * jax.random.normal(key_list[8], (HEADS * HD,), jnp.float32), 0.25, 1.75).astype(jnp.bfloat16)
    return {"lin_q": lin_q, "lin_k": lin_k, "lin_v": lin_v, "att_q": att_q, "att_k": att_k, "att_v": att_v, "block_lists": block_lists, "gain_lin": gain_lin, "gain_att": gain_att}


epsilon = 1e-06

def linear_mixer(lin_q, lin_k, lin_v):
    query_blocks = lin_q.reshape(NBLK, BLK, HEADS, HD)
    key_blocks = lin_k.reshape(NBLK, BLK, HEADS, HD)
    value_blocks = lin_v.reshape(NBLK, BLK, HEADS, HD)
    lower = jnp.arange(BLK)[:, None] >= jnp.arange(BLK)[None, :]

    def advance(state, pieces):
        query_blk = pieces[0].astype(jnp.float32)
        key_blk = pieces[1].astype(jnp.float32)
        value_blk = pieces[2].astype(jnp.float32)
        scores = jnp.einsum('thd,shd->hts', query_blk, key_blk)
        scores = lax.optimization_barrier(jnp.where(lower[None], scores, 0.0).astype(jnp.bfloat16))
        intra = jnp.einsum('hts,shd->thd', scores.astype(jnp.float32), value_blk)
        carried_low = lax.optimization_barrier(state.astype(jnp.bfloat16))
        inter = jnp.einsum('thd,hde->the', query_blk, carried_low.astype(jnp.float32))
        state = state + jnp.einsum('shd,she->hde', key_blk, value_blk)
        return (state, intra + inter)
    initial = jnp.zeros((HEADS, HD, HD), jnp.float32)
    final_state, outputs = lax.scan(advance, initial, (query_blocks, key_blocks, value_blocks))
    return outputs.reshape(SEQ, HEADS * HD)

def tree_attention(att_q, att_k, att_v, block_lists):
    groups = HEADS // KV_HEADS
    score_scale = HD ** (-0.5)
    padding = jnp.zeros(((SPAN - 1) * BLK, KV_HEADS * HD), att_k.dtype)
    keys_padded = jnp.concatenate([padding, att_k], axis=0)
    values_padded = jnp.concatenate([padding, att_v], axis=0)

    def one_block(block):
        start = (block * BLK).astype(jnp.int32)
        queries = lax.dynamic_slice_in_dim(att_q, start, BLK, 0).astype(jnp.float32).reshape(BLK, KV_HEADS, groups, HD)
        keys_win = lax.dynamic_slice_in_dim(keys_padded, start, SPAN * BLK, 0).astype(jnp.float32).reshape(SPAN * BLK, KV_HEADS, HD)
        values_win = lax.dynamic_slice_in_dim(values_padded, start, SPAN * BLK, 0).astype(jnp.float32).reshape(SPAN * BLK, KV_HEADS, HD)
        key_index = jnp.arange(SPAN * BLK, dtype=jnp.int32)
        key_block = block - (SPAN - 1) + key_index // BLK
        entries = block_lists[block]
        listed = jnp.any(entries[None, :] == key_block[:, None], axis=1) & (key_block >= 0)
        query_pos = block * BLK + jnp.arange(BLK, dtype=jnp.int32)
        key_pos = (block - (SPAN - 1)) * BLK + key_index
        allowed = listed[None, :] & (key_pos[None, :] <= query_pos[:, None])
        scores = jnp.einsum('tgqd,sgd->gqts', queries, keys_win) * score_scale
        scores = jnp.where(allowed[None, None], scores, -1e+30)
        row_max = lax.optimization_barrier(jnp.max(scores, axis=-1, keepdims=True))
        expo = jnp.exp(scores - row_max)
        weights = (expo / lax.optimization_barrier(jnp.sum(expo, axis=-1, keepdims=True))).astype(jnp.bfloat16)
        attended = jnp.einsum('gqts,sgd->tgqd', weights.astype(jnp.float32), values_win)
        return attended.reshape(BLK, HEADS * HD)
    outputs = lax.map(one_block, jnp.arange(NBLK, dtype=jnp.int32))
    return outputs.reshape(SEQ, HEADS * HD)

def reference(lin_q, lin_k, lin_v, att_q, att_k, att_v, block_lists, gain_lin, gain_att):
    lin_out = linear_mixer(lin_q, lin_k, lin_v)
    att_out = tree_attention(att_q, att_k, att_v, block_lists)
    lin_norm = lin_out / jnp.sqrt(lax.optimization_barrier(jnp.mean(lin_out * lin_out, axis=1, keepdims=True)) + epsilon)
    att_norm = att_out / jnp.sqrt(lax.optimization_barrier(jnp.mean(att_out * att_out, axis=1, keepdims=True)) + epsilon)
    mixed = lin_norm * gain_lin.astype(jnp.float32)[None, :] + att_norm * gain_att.astype(jnp.float32)[None, :]
    return mixed.astype(jnp.bfloat16)
```

```python
import functools
import math

import jax
import jax.numpy as jnp
from jax import lax
from jax.experimental import pallas as pl
from jax.experimental.pallas import tpu as pltpu
from jax.sharding import PartitionSpec as P

HD = 128
BLK = 128
SPAN = 5
EPS = 1e-06
NEG = -1e30
MESH = pl.DeviceIdType.MESH
BF16, F32 = jnp.bfloat16, jnp.float32


def dot(a, b, dims):
    return lax.dot_general(a, b, (dims, ((), ())), preferred_element_type=F32)


def kernel(
    n, nt, lists, lin_q_h, lin_k_h, lin_v_h, att_q_h, att_k_h, att_v_h, gain_lin_h, gain_att_h,
    out, lin_q, lin_k, lin_v, att_q, att_k, att_v, gain_lin, gain_att, kv, home, pre, first, scores, lin_out, att_out,
    xout, xin, zout, zin, bout, bin_, pback, sq_out, sq_in,
    lsem, kvs, kvr, hs_, hr, xs, xr, zs, zr, bs, br, ps, pr, ns, nr,
):
    ctx, tp = lax.axis_index("ctx"), lax.axis_index("tp")
    p, o = lax.rem(ctx, 2), lax.div(ctx, 2)
    core = lax.rem(tp, 2)
    chief, left = tp + 1 - core, tp - core
    lead = core == 1
    mate = ctx + 1 - 2 * p
    tokens = lin_q.shape[0]
    heads = lin_q.shape[1] // HD
    kv_heads = att_k.shape[1] // HD
    half = heads // 2
    has_prev, has_next = o > 0, o < n // 2 - 1
    side, ahead, behind = {"ctx": mate}, {"ctx": ctx + 2}, {"ctx": ctx - 2}

    pairs = (
        (lin_k_h, lin_k), (lin_v_h, lin_v), (lin_q_h, lin_q),
        (att_q_h, att_q), (att_k_h, att_k), (att_v_h, att_v),
        (gain_lin_h, gain_lin), (gain_att_h, gain_att),
    )
    local = [pltpu.make_async_copy(s, d, lsem.at[i]) for i, (s, d) in enumerate(pairs)]
    barrier = pltpu.get_barrier_semaphore()

    def greet(where):
        pl.semaphore_signal(barrier, inc=1, device_id=where, device_id_type=MESH)

    greet({"ctx": mate, "tp": left})
    greet({"ctx": mate, "tp": chief})
    pl.when(has_prev)(lambda: greet(behind))
    pl.when(has_next)(lambda: greet(ahead))
    for k in range(1, nt):
        greet({"tp": lax.rem(tp + k, nt)})
    for c in local:
        c.start()

    def remote(src, dst, ssem, rsem, where):
        return pltpu.make_async_remote_copy(
            src_ref=src, dst_ref=dst, send_sem=ssem, recv_sem=rsem,
            device_id=where, device_id_type=MESH,
        )

    def kv_copies(src, slot, sem, where):
        return [
            [
                remote(
                    src[a].at[:, pl.ds(g * HD, HD)], kv.at[slot, a, :, pl.ds(g * HD, HD)],
                    kvs.at[sem, g, a], kvr.at[sem, g, a], where,
                )
                for a in range(2)
            ]
            for g in range(kv_heads)
        ]

    kv_src = (att_k_h, att_v_h)
    kv_ahead = kv_copies(kv_src, 1, 1, ahead)
    kv_side = kv_copies(kv_src, 0, 0, side)
    kv_pass = kv_copies((kv.at[1, 0], kv.at[1, 1]), 0, 0, side)

    def send_kv(g):
        for a in range(2):
            pl.when(has_next)(kv_ahead[g][a].start)
            pl.when(p == 0)(kv_side[g][a].start)

    def sent_kv(g):
        for a in range(2):
            pl.when(has_next)(kv_ahead[g][a].wait_send)
            pl.when(p == 0)(kv_side[g][a].wait_send)

    def lanes(h):
        return pl.ds(pl.multiple_of(h * HD, HD), HD)

    x_copy = [
        remote(xout.at[j], xin.at[core, j], xs.at[j], xr.at[core, j], {"ctx": mate, "tp": chief})
        for j in range(half)
    ]
    x_recv = [
        [remote(xout.at[j], xin.at[c, j], xs.at[j], xr.at[c, j], side) for j in range(half)]
        for c in range(2)
    ]
    h_copy = [
        remote(home.at[0, j], home.at[0, j], hs_.at[j], hr.at[j], {"tp": chief})
        for j in range(half)
    ]
    z_copy = [
        [remote(zout.at[c, j], zin.at[c, j], zs.at[c, j], zr.at[c, j], ahead) for j in range(half)]
        for c in range(2)
    ]
    b_copy = [
        [
            remote(bout.at[c, j], bin_.at[j], bs.at[c, j], br.at[j], {"ctx": mate, "tp": left + c})
            for j in range(half)
        ]
        for c in range(2)
    ]
    p_copy = [
        remote(pback.at[j], pre.at[j], ps.at[j], pr.at[j], {"tp": left}) for j in range(half)
    ]
    other, mine = (1 - p) * half, p * half

    local[0].wait()
    local[1].wait()
    for j in range(half):
        h = other + j
        xout[j] = dot(lin_k[:, lanes(h)], lin_v[:, lanes(h)], ((0,), (0,))).astype(BF16)
    for j in range(half):
        h = mine + j
        home[core, j] = dot(lin_k[:, lanes(h)], lin_v[:, lanes(h)], ((0,), (0,)))

    @pl.when(jnp.logical_not(has_prev))
    def _():
        kv[1] = jnp.zeros_like(kv[1])

        @pl.when(p == 0)
        def _():
            kv[0] = jnp.zeros_like(kv[0])
            bin_[...] = jnp.zeros_like(bin_)

    pl.semaphore_wait(barrier, nt + 1 + has_prev.astype(jnp.int32) + has_next.astype(jnp.int32))

    send_x = (p == 0) | has_next
    take_x = (p == 1) | has_next
    send_b = (p == 0) | has_prev
    take_b = (p == 1) | has_prev

    def start_x():
        for j in range(half):
            x_copy[j].start()

    @pl.when(jnp.logical_not(lead))
    def _():
        for j in range(half):
            h_copy[j].start()

    pl.when(send_x & (o < 2))(start_x)
    send_kv(0)
    pl.when(send_x & (o >= 2) & has_next)(start_x)

    local[2].wait()
    row = lax.broadcasted_iota(jnp.int32, (BLK, BLK), 0)
    col = lax.broadcasted_iota(jnp.int32, (BLK, BLK), 1)
    lower = row >= col
    blocks = tokens // BLK
    for h in range(heads):
        hs = pl.ds(h * HD, HD)
        for b in range(blocks):
            rows = pl.ds(b * BLK, BLK)
            s = dot(lin_q[rows, hs], lin_k[rows, hs], ((1,), (1,)))
            scores[rows, hs] = jnp.where(lower, s, 0.0).astype(BF16)
        first[h] = dot(lin_k[0:BLK, hs], lin_v[0:BLK, hs], ((0,), (0,)))

    def forward(g, a):
        @pl.when(has_prev)
        def _():
            kv_ahead[g][a].wait_recv()
            pl.when(p == 1)(kv_pass[g][a].start)

    def link(c, j):
        @pl.when(has_prev)
        def _():
            z_copy[c][j].wait_recv()

        @pl.when(jnp.logical_not(has_prev))
        def _():
            zin[c, j] = jnp.zeros_like(zin[c, j])

        if c == 0:
            h_copy[j].wait_recv()
        before, here = zin[c, j].astype(F32), home[c, j]
        @pl.when(has_next)
        def _():
            x_recv[c][j].wait_recv()
            zout[c, j] = (before + here + xin[c, j].astype(F32)).astype(BF16)
            z_copy[c][j].start()
        bout[c, j] = jnp.where(p == 0, before + here, before).astype(BF16)
        pl.when(send_b)(b_copy[c][j].start)
        back = pback if c == 0 else pre

        @pl.when(p == 0)
        def _():
            back[j] = before

        @pl.when(p == 1)
        def _():
            pl.when(jnp.logical_not(has_next))(x_recv[c][j].wait_recv)
            back[j] = before + xin[c, j].astype(F32)

        if c == 0:
            p_copy[j].start()

    quarter = half // 2
    steps = [(1, j) for j in range(quarter)] + [(0, j) for j in range(half)] + [(1, j) for j in range(quarter, half)]
    passes = [(g, a) for g in range(kv_heads) for a in range(2)]

    def chain():
        for c, j in steps:
            link(c, j)

    def weave(at):
        for i, (c, j) in enumerate(steps):
            for k, (g, a) in enumerate(passes):
                if at[min(k, len(at) - 1)] == i:
                    forward(g, a)
            link(c, j)

    pl.when(lead & jnp.logical_not(has_prev))(chain)
    for g in range(1, kv_heads):
        sent_kv(g - 1)
        send_kv(g)
    pl.when(send_x & (o >= 2) & jnp.logical_not(has_next))(start_x)
    inner = lead & has_prev & has_next
    pl.when(inner & (o < 2))(lambda: weave((0, 2, 5, 7)))
    pl.when(inner & (o >= 2))(lambda: weave((0, 0, 1, 5)))
    outer = jnp.logical_not(inner)

    for c in local[3:]:
        c.wait()
    factor = (HD ** -0.5) * math.log2(math.e)
    bias = []
    for b in range(blocks):
        parts = []
        for i in range(SPAN - 1):
            key_block = ctx * blocks + b - (SPAN - 1) + i
            hit = lists[b, 0] == key_block
            for e in range(1, 4):
                hit = hit | (lists[b, e] == key_block)
            value = jnp.where(hit & (key_block >= 0), 0.0, NEG).astype(F32)
            parts.append(jnp.full((1, BLK), value, F32))
        bias.append(parts)

    att_sq = [None] * blocks
    kept = {}

    def group_of(g):
        return range(g * heads // kv_heads, (g + 1) * heads // kv_heads)

    def queries_of(g, b):
        rows = pl.ds(b * BLK, BLK)
        return jnp.concatenate([att_q[rows, pl.ds(h * HD, HD)] for h in group_of(g)], axis=0)

    def attend_near(g):
        gs = pl.ds(g * HD, HD)
        for b in range(blocks):
            rows = pl.ds(b * BLK, BLK)

            def window(a, own):
                return jnp.concatenate([kv[1, a, b * BLK:, gs], own[: (b + 1) * BLK, gs]], axis=0)

            keys, values = window(0, att_k), window(1, att_v)
            sall = dot(queries_of(g, b), keys, ((1,), (1,)))
            cut = sall.shape[1] - BLK
            add = jnp.concatenate(bias[b][: blocks - b] + bias[b][2 * blocks - b:], axis=1)
            wall = []
            for i in range(len(group_of(g))):
                s = sall[i * BLK:(i + 1) * BLK]
                s = jnp.concatenate([s[:, :cut] + add, jnp.where(lower, s[:, cut:], NEG)], axis=1)
                m = jnp.max(s, axis=1, keepdims=True)
                e = jnp.exp2((s - m) * factor)
                kept[g, b, i] = (m, jnp.sum(e, axis=1, keepdims=True))
                wall.append(e.astype(BF16))
            rall = dot(jnp.concatenate(wall, axis=0), values, ((1,), (0,)))
            for i, h in enumerate(group_of(g)):
                att_out[rows, pl.ds(h * HD, HD)] = rall[i * BLK:(i + 1) * BLK]

    def attend_far(g):
        gs = pl.ds(g * HD, HD)
        for a in range(2):
            pl.when((p == 1) | has_prev)(kv_side[g][a].wait_recv)
        for b in range(blocks):
            rows = pl.ds(b * BLK, BLK)
            sall = dot(queries_of(g, b), kv[0, 0, :, gs], ((1,), (1,)))
            add = jnp.concatenate(bias[b][blocks - b: 2 * blocks - b], axis=1)
            wall, scale = [], []
            for i in range(len(group_of(g))):
                m_near, l_near = kept[g, b, i]
                s = sall[i * BLK:(i + 1) * BLK] + add
                m = jnp.maximum(m_near, jnp.max(s, axis=1, keepdims=True))
                e = jnp.exp2((s - m) * factor)
                keep = jnp.exp2((m_near - m) * factor)
                inv = 1.0 / (keep * l_near + jnp.sum(e, axis=1, keepdims=True))
                scale.append((keep * inv, inv))
                wall.append(e.astype(BF16))
            rall = dot(jnp.concatenate(wall, axis=0), kv[0, 1, :, gs], ((1,), (0,)))
            for i, h in enumerate(group_of(g)):
                hs = pl.ds(h * HD, HD)
                r = att_out[rows, hs] * scale[i][0] + rall[i * BLK:(i + 1) * BLK] * scale[i][1]
                att_out[rows, hs] = r
                att_sq[b] = r * r if att_sq[b] is None else att_sq[b] + r * r

    for g in range(kv_heads):
        @pl.when(outer)
        def _():
            for a in range(2):
                forward(g, a)
        attend_near(g)
    pl.when(lead & has_prev & jnp.logical_not(has_next))(chain)
    for g in range(kv_heads):
        attend_far(g)
    lin_sq = [None] * blocks

    def finish(h, prefix):
        for b in range(blocks):
            rows = pl.ds(b * BLK, BLK)
            low = (prefix if b == 0 else prefix + first[h]).astype(BF16)
            lhs = jnp.concatenate([scores[rows, lanes(h)], lin_q[rows, lanes(h)]], axis=1)
            rhs = jnp.concatenate([lin_v[rows, lanes(h)], low], axis=0)
            r = dot(lhs, rhs, ((1,), (0,)))
            lin_out[rows, lanes(h)] = r
            lin_sq[b] = r * r if lin_sq[b] is None else lin_sq[b] + r * r

    for j in range(half):
        pl.when(jnp.logical_not(lead))(p_copy[j].wait_recv)
        finish(mine + j, pre[j])
    for j in range(half):
        pl.when(take_b)(b_copy[0][j].wait_recv)
        finish(other + j, bin_[j].astype(F32))

    def as_row(parts):
        return jnp.sum(jnp.concatenate(parts, axis=0).T, axis=0, keepdims=True)

    top = lax.broadcasted_iota(jnp.int32, (8, tokens), 0) == 0
    sums = jnp.where(top, as_row(lin_sq), as_row(att_sq))
    sq_out[...] = sums
    n_copy = [
        remote(sq_out, sq_in.at[k - 1], ns.at[k - 1], nr.at[k - 1], {"tp": lax.rem(tp + k, nt)})
        for k in range(1, nt)
    ]
    for c in n_copy:
        c.start()
    sent_kv(kv_heads - 1)

    @pl.when((p == 1) & has_prev)
    def _():
        for g in range(kv_heads):
            for a in range(2):
                kv_pass[g][a].wait_send()

    for j in range(half):
        pl.when(send_x)(x_copy[j].wait_send)
        pl.when(jnp.logical_not(lead))(h_copy[j].wait_send)

    @pl.when(lead)
    def _():
        for c in range(2):
            for j in range(half):
                pl.when(has_next)(z_copy[c][j].wait_send)
                pl.when(send_b)(b_copy[c][j].wait_send)
        for j in range(half):
            p_copy[j].wait_send()

    for k in range(nt - 1):
        n_copy[k].wait_recv()
        sums = sums + sq_in[k]
    inv = lax.rsqrt(sums * (1.0 / (nt * heads * HD)) + EPS)

    def as_column(r):
        return jnp.broadcast_to(r, (HD, tokens)).T

    lin_inv, att_inv = as_column(inv[0:1]), as_column(inv[1:2])
    gl, ga = gain_lin[...].astype(F32), gain_att[...].astype(F32)
    for h in range(heads):
        hs = pl.ds(h * HD, HD)
        out[:, hs] = (
            lin_out[:, hs] * lin_inv * gl[h:h + 1] + att_out[:, hs] * att_inv * ga[h:h + 1]
        ).astype(BF16)
    for c in n_copy:
        c.wait_send()


def per_device(n, nt, lin_q, lin_k, lin_v, att_q, att_k, att_v, block_lists, gain_lin, gain_att):
    tokens, columns = lin_q.shape
    heads, half = columns // HD, columns // HD // 2
    gain_lin, gain_att = gain_lin.reshape(heads, HD), gain_att.reshape(heads, HD)
    anywhere = pl.BlockSpec(memory_space=pl.ANY)
    wide, kv_wide = (tokens, columns), att_k.shape
    state, kv_heads = (half, HD, HD), kv_wide[1] // HD
    dma = pltpu.SemaphoreType.DMA
    return pl.pallas_call(
        functools.partial(kernel, n, nt),
        out_shape=pltpu.VMEM(wide, BF16),
        in_specs=[pl.BlockSpec(memory_space=pltpu.SMEM)] + [anywhere] * 8,
        out_specs=pl.BlockSpec(memory_space=pltpu.VMEM),
        scratch_shapes=[
            pltpu.VMEM(wide, BF16), pltpu.VMEM(wide, BF16), pltpu.VMEM(wide, BF16),
            pltpu.VMEM(wide, BF16), pltpu.VMEM(kv_wide, BF16), pltpu.VMEM(kv_wide, BF16),
            pltpu.VMEM((heads, HD), BF16), pltpu.VMEM((heads, HD), BF16),
            pltpu.VMEM((2, 2) + kv_wide, BF16),
            pltpu.VMEM((2,) + state, F32), pltpu.VMEM(state, F32), pltpu.VMEM((heads, HD, HD), F32),
            pltpu.VMEM(wide, BF16), pltpu.VMEM(wide, F32), pltpu.VMEM(wide, F32),
            pltpu.VMEM(state, BF16), pltpu.VMEM((2,) + state, BF16),
            pltpu.VMEM((2,) + state, BF16), pltpu.VMEM((2,) + state, BF16),
            pltpu.VMEM((2,) + state, BF16), pltpu.VMEM(state, BF16), pltpu.VMEM(state, F32),
            pltpu.VMEM((8, tokens), F32), pltpu.VMEM((nt - 1, 8, tokens), F32),
            dma((8,)), dma((2, kv_heads, 2)), dma((2, kv_heads, 2)),
            dma((half,)), dma((half,)),
            dma((half,)), dma((2, half)), dma((2, half)), dma((2, half)),
            dma((2, half)), dma((half,)), dma((half,)), dma((half,)),
            dma((nt - 1,)), dma((nt - 1,)),
        ],
        compiler_params=pltpu.CompilerParams(
            collective_id=0, has_side_effects=True, vmem_limit_bytes=63 * 2 ** 20
        ),
    )(block_lists, lin_q, lin_k, lin_v, att_q, att_k, att_v, gain_lin, gain_att)


def solution(mesh):
    wide = P("ctx", "tp")
    return jax.shard_map(
        functools.partial(per_device, mesh.shape["ctx"], mesh.shape["tp"]),
        mesh=mesh,
        in_specs=(wide,) * 6 + (P("ctx", None), P("tp"), P("tp")),
        out_specs=wide,
        check_vma=False,
    )
```

```python
import functools
import math

import jax
import jax.numpy as jnp
from jax import lax
from jax.experimental import pallas as pl
from jax.experimental.pallas import tpu as pltpu
from jax.sharding import PartitionSpec as P

HD = 128
BLK = 128
SPAN = 5
EPS = 1e-06
NEG = -1e30
MESH = pl.DeviceIdType.MESH
BF16, F32 = jnp.bfloat16, jnp.float32


def dot(a, b, dims):
    return lax.dot_general(a, b, (dims, ((), ())), preferred_element_type=F32)


def kernel(
    n, nt, lists, lin_q_h, lin_k_h, lin_v_h, att_q_h, att_k_h, att_v_h, gain_lin_h, gain_att_h,
    out, lin_q, lin_k, lin_v, att_q, att_k, att_v, gain_lin, gain_att, kv, home, pre, first, scores, lin_out, att_out,
    xout, xin, zout, zin, bout, bin_, pback, squares, sq_out, sq_in,
    lsem, kvs, kvr, hs_, hr, xs, xr, zs, zr, bs, br, ps, pr, ns, nr,
):
    ctx, tp = lax.axis_index("ctx"), lax.axis_index("tp")
    p, o = lax.rem(ctx, 2), lax.div(ctx, 2)
    core = lax.rem(tp, 2)
    chief, left = tp + 1 - core, tp - core
    lead = core == 1
    mate = ctx + 1 - 2 * p
    tokens = lin_q.shape[0]
    heads = lin_q.shape[1] // HD
    kv_heads = att_k.shape[1] // HD
    half = heads // 2
    has_prev, has_next = o > 0, o < n // 2 - 1
    side, ahead, behind = {"ctx": mate}, {"ctx": ctx + 2}, {"ctx": ctx - 2}

    pairs = (
        (lin_k_h, lin_k), (lin_v_h, lin_v), (lin_q_h, lin_q),
        (att_q_h, att_q), (att_k_h, att_k), (att_v_h, att_v),
        (gain_lin_h, gain_lin), (gain_att_h, gain_att),
    )
    local = [pltpu.make_async_copy(s, d, lsem.at[i]) for i, (s, d) in enumerate(pairs)]
    barrier = pltpu.get_barrier_semaphore()

    def greet(where):
        pl.semaphore_signal(barrier, inc=1, device_id=where, device_id_type=MESH)

    greet({"ctx": mate, "tp": left})
    greet({"ctx": mate, "tp": chief})
    pl.when(has_prev)(lambda: greet(behind))
    pl.when(has_next)(lambda: greet(ahead))
    for k in range(1, nt):
        greet({"tp": lax.rem(tp + k, nt)})
    for c in local:
        c.start()

    def remote(src, dst, ssem, rsem, where):
        return pltpu.make_async_remote_copy(
            src_ref=src, dst_ref=dst, send_sem=ssem, recv_sem=rsem,
            device_id=where, device_id_type=MESH,
        )

    pieces = [(0, 0, 0, tokens), (0, 1, 0, tokens), (1, 0, 0, tokens), (1, 1, 0, tokens // 2), (1, 1, tokens // 2, tokens // 2)]

    def kv_copies(src, slot, sem, where):
        return [
            remote(
                src[a].at[pl.ds(r, m), pl.ds(g * HD, HD)], kv.at[slot, a, pl.ds(r, m), pl.ds(g * HD, HD)],
                kvs.at[sem, i], kvr.at[sem, i], where,
            )
            for i, (g, a, r, m) in enumerate(pieces)
        ]

    kv_src = (att_k_h, att_v_h)
    kv_ahead = kv_copies(kv_src, 1, 1, ahead)
    kv_side = kv_copies(kv_src, 0, 0, side)
    kv_pass = kv_copies((kv.at[1, 0], kv.at[1, 1]), 0, 0, side)
    which = range(len(pieces))

    def send_ahead(ids):
        for i in ids:
            pl.when(has_next)(kv_ahead[i].start)

    def send_side(ids):
        for i in ids:
            pl.when(p == 0)(kv_side[i].start)

    def lanes(h):
        return pl.ds(pl.multiple_of(h * HD, HD), HD)

    x_copy = [
        remote(xout.at[j], xin.at[core, j], xs.at[j], xr.at[core, j], {"ctx": mate, "tp": chief})
        for j in range(half)
    ]
    x_recv = [
        [remote(xout.at[j], xin.at[c, j], xs.at[j], xr.at[c, j], side) for j in range(half)]
        for c in range(2)
    ]
    h_copy = [
        remote(home.at[0, j], home.at[0, j], hs_.at[j], hr.at[j], {"tp": chief})
        for j in range(half)
    ]
    z_copy = [
        [remote(zout.at[c, j], zin.at[c, j], zs.at[c, j], zr.at[c, j], ahead) for j in range(half)]
        for c in range(2)
    ]
    b_copy = [
        [
            remote(bout.at[c, j], bin_.at[j], bs.at[c, j], br.at[j], {"ctx": mate, "tp": left + c})
            for j in range(half)
        ]
        for c in range(2)
    ]
    p_copy = [
        remote(pback.at[j], pre.at[j], ps.at[j], pr.at[j], {"tp": left}) for j in range(half)
    ]
    other, mine = (1 - p) * half, p * half

    local[0].wait()
    local[1].wait()
    for j in range(half):
        h = other + j
        xout[j] = dot(lin_k[:, lanes(h)], lin_v[:, lanes(h)], ((0,), (0,))).astype(BF16)
    for j in range(half):
        h = mine + j
        home[core, j] = dot(lin_k[:, lanes(h)], lin_v[:, lanes(h)], ((0,), (0,)))

    @pl.when(jnp.logical_not(has_prev))
    def _():
        kv[1] = jnp.zeros_like(kv[1])

        @pl.when(p == 0)
        def _():
            kv[0] = jnp.zeros_like(kv[0])
            bin_[...] = jnp.zeros_like(bin_)

    pl.semaphore_wait(barrier, nt + 1 + has_prev.astype(jnp.int32) + has_next.astype(jnp.int32))

    send_x = (p == 0) | has_next
    take_x = (p == 1) | has_next
    send_b = (p == 0) | has_prev
    take_b = (p == 1) | has_prev

    def start_x():
        for j in range(half):
            x_copy[j].start()

    @pl.when(jnp.logical_not(lead))
    def _():
        for j in range(half):
            h_copy[j].start()

    rest = which[2:]
    pl.when(send_x & (o < 2))(start_x)
    send_ahead((0,))
    pl.when((o > 0) | jnp.logical_not(lead))(lambda: send_ahead((1,)))
    send_side((0, 1))
    pl.when((o > 0) | jnp.logical_not(lead))(lambda: send_ahead((2,)))
    pl.when((o > 1) | (o == 1) & jnp.logical_not(lead))(lambda: send_ahead((3, 4)))
    pl.when(send_x & (o >= 2) & has_next)(start_x)
    send_side(rest)
    pl.when(send_x & (o >= 2) & jnp.logical_not(has_next))(start_x)

    local[2].wait()
    row = lax.broadcasted_iota(jnp.int32, (BLK, BLK), 0)
    col = lax.broadcasted_iota(jnp.int32, (BLK, BLK), 1)
    lower = row >= col
    blocks = tokens // BLK
    for h in range(heads):
        hs = pl.ds(h * HD, HD)
        for b in range(blocks):
            rows = pl.ds(b * BLK, BLK)
            s = dot(lin_q[rows, hs], lin_k[rows, hs], ((1,), (1,)))
            scores[rows, hs] = jnp.where(lower, s, 0.0).astype(BF16)
        first[h] = dot(lin_k[0:BLK, hs], lin_v[0:BLK, hs], ((0,), (0,)))

    def forward(ids):
        @pl.when(has_prev)
        def _():
            for i in ids:
                kv_ahead[i].wait_recv()
                pl.when(p == 1)(kv_pass[i].start)

    def link(c, j):
        @pl.when(has_prev)
        def _():
            z_copy[c][j].wait_recv()

        @pl.when(jnp.logical_not(has_prev))
        def _():
            zin[c, j] = jnp.zeros_like(zin[c, j])

        if c == 0:
            h_copy[j].wait_recv()
        before, here = zin[c, j].astype(F32), home[c, j]
        @pl.when(has_next)
        def _():
            x_recv[c][j].wait_recv()
            zout[c, j] = (before + here + xin[c, j].astype(F32)).astype(BF16)
            z_copy[c][j].start()
        bout[c, j] = jnp.where(p == 0, before + here, before).astype(BF16)
        pl.when(send_b)(b_copy[c][j].start)
        back = pback if c == 0 else pre

        @pl.when(p == 0)
        def _():
            back[j] = before

        @pl.when(p == 1)
        def _():
            pl.when(jnp.logical_not(has_next))(x_recv[c][j].wait_recv)
            back[j] = before + xin[c, j].astype(F32)

        if c == 0:
            p_copy[j].start()

    quarter = half // 2
    steps = [(1, j) for j in range(quarter)] + [(0, j) for j in range(half)] + [(1, j) for j in range(quarter, half)]

    def chain():
        for c, j in steps:
            link(c, j)

    def weave(at, then=lambda: None):
        for i, (c, j) in enumerate(steps):
            forward([k for k in which if at[k] == i])
            link(c, j)
        then()
        forward([k for k in which if at[k] >= len(steps)])

    inner = lead & has_prev & has_next
    outer = jnp.logical_not(inner)
    back_early = jnp.logical_not(lead) & (o < 2)

    @pl.when(lead & jnp.logical_not(has_prev))
    def _():
        chain()
        send_ahead((1, 2, 3, 4))

    @pl.when(inner & (o < 2))
    def _():
        weave((0, 8, 8, 8, 8), lambda: send_ahead((3, 4)))


    def late_kv():
        for j in range(half):
            p_copy[j].wait_recv()
        pl.when(o == 0)(lambda: send_ahead((3, 4)))

    for c in local[3:]:
        c.wait()
    factor = (HD ** -0.5) * math.log2(math.e)
    bias = []
    for b in range(blocks):
        parts = []
        for i in range(SPAN - 1):
            key_block = ctx * blocks + b - (SPAN - 1) + i
            hit = lists[b, 0] == key_block
            for e in range(1, 4):
                hit = hit | (lists[b, e] == key_block)
            value = jnp.where(hit & (key_block >= 0), 0.0, NEG).astype(F32)
            parts.append(jnp.full((1, BLK), value, F32))
        bias.append(parts)

    kept = {}

    def group_of(g):
        return range(g * heads // kv_heads, (g + 1) * heads // kv_heads)

    def queries_of(g, b):
        rows = pl.ds(b * BLK, BLK)
        return jnp.concatenate([att_q[rows, pl.ds(h * HD, HD)] for h in group_of(g)], axis=0)

    def attend_near(g):
        gs = pl.ds(g * HD, HD)
        for b in range(blocks):
            rows = pl.ds(b * BLK, BLK)

            def window(a, own):
                return jnp.concatenate([kv[1, a, b * BLK:, gs], own[: (b + 1) * BLK, gs]], axis=0)

            keys, values = window(0, att_k), window(1, att_v)
            sall = dot(queries_of(g, b), keys, ((1,), (1,)))
            cut = sall.shape[1] - BLK
            add = jnp.concatenate(bias[b][: blocks - b] + bias[b][2 * blocks - b:], axis=1)
            wall = []
            for i in range(len(group_of(g))):
                s = sall[i * BLK:(i + 1) * BLK]
                s = jnp.concatenate([s[:, :cut] + add, jnp.where(lower, s[:, cut:], NEG)], axis=1)
                m = jnp.max(s, axis=1, keepdims=True)
                e = jnp.exp2((s - m) * factor)
                kept[g, b, i] = (m, jnp.sum(e, axis=1, keepdims=True))
                wall.append(e.astype(BF16))
            rall = dot(jnp.concatenate(wall, axis=0), values, ((1,), (0,)))
            for i, h in enumerate(group_of(g)):
                att_out[rows, pl.ds(h * HD, HD)] = rall[i * BLK:(i + 1) * BLK]

    def attend_far(g):
        gs = pl.ds(g * HD, HD)
        for i in which:
            if pieces[i][0] == g:
                pl.when((p == 1) | has_prev)(kv_side[i].wait_recv)
        for b in range(blocks):
            rows = pl.ds(b * BLK, BLK)
            sall = dot(queries_of(g, b), kv[0, 0, :, gs], ((1,), (1,)))
            add = jnp.concatenate(bias[b][blocks - b: 2 * blocks - b], axis=1)
            wall, scale = [], []
            for i in range(len(group_of(g))):
                m_near, l_near = kept[g, b, i]
                s = sall[i * BLK:(i + 1) * BLK] + add
                m = jnp.maximum(m_near, jnp.max(s, axis=1, keepdims=True))
                e = jnp.exp2((s - m) * factor)
                keep = jnp.exp2((m_near - m) * factor)
                inv = 1.0 / (keep * l_near + jnp.sum(e, axis=1, keepdims=True))
                scale.append((keep * inv, inv))
                wall.append(e.astype(BF16))
            rall = dot(jnp.concatenate(wall, axis=0), kv[0, 1, :, gs], ((1,), (0,)))
            sq = None if g == 0 else squares[1, rows]
            for i, h in enumerate(group_of(g)):
                hs = pl.ds(h * HD, HD)
                r = att_out[rows, hs] * scale[i][0] + rall[i * BLK:(i + 1) * BLK] * scale[i][1]
                att_out[rows, hs] = r
                sq = r * r if sq is None else sq + r * r
            squares[1, rows] = sq

    def finish(h, prefix, fresh):
        for b in range(blocks):
            rows = pl.ds(b * BLK, BLK)
            low = (prefix if b == 0 else prefix + first[h]).astype(BF16)
            lhs = jnp.concatenate([scores[rows, lanes(h)], lin_q[rows, lanes(h)]], axis=1)
            rhs = jnp.concatenate([lin_v[rows, lanes(h)], low], axis=0)
            r = dot(lhs, rhs, ((1,), (0,)))
            lin_out[rows, lanes(h)] = r
            squares[0, rows] = r * r if fresh else squares[0, rows] + r * r

    def finish_mine():
        for j in range(half):
            pl.when(jnp.logical_not(lead) & (o >= 2))(p_copy[j].wait_recv)
            finish(mine + j, pre[j], j == 0)

    pl.when(outer | (o >= 2))(lambda: forward((0, 1)))
    attend_near(0)
    pl.when(inner & (o >= 2))(lambda: weave((-1, -1, 0, 8, 8)))
    pl.when(back_early)(late_kv)
    pl.when(o < 2)(finish_mine)
    pl.when(p == 0)(lambda: attend_far(0))
    pl.when(outer)(lambda: forward((2, 3, 4)))
    attend_near(1)
    pl.when(lead & has_prev & jnp.logical_not(has_next))(chain)
    pl.when(p == 1)(lambda: attend_far(0))
    attend_far(1)
    pl.when(o >= 2)(finish_mine)
    for j in range(half):
        pl.when(take_b)(b_copy[0][j].wait_recv)
        finish(other + j, bin_[j].astype(F32), False)

    def as_row(sq):
        return jnp.sum(sq.T, axis=0, keepdims=True)

    top = lax.broadcasted_iota(jnp.int32, (8, tokens), 0) == 0
    sums = jnp.where(top, as_row(squares[0]), as_row(squares[1]))
    sq_out[...] = sums
    n_copy = [
        remote(sq_out, sq_in.at[k - 1], ns.at[k - 1], nr.at[k - 1], {"tp": lax.rem(tp + k, nt)})
        for k in range(1, nt)
    ]
    for c in n_copy:
        c.start()
    for i in which:
        pl.when(has_next)(kv_ahead[i].wait_send)
        pl.when(p == 0)(kv_side[i].wait_send)

    @pl.when((p == 1) & has_prev)
    def _():
        for i in which:
            kv_pass[i].wait_send()

    for j in range(half):
        pl.when(send_x)(x_copy[j].wait_send)
        pl.when(jnp.logical_not(lead))(h_copy[j].wait_send)

    @pl.when(lead)
    def _():
        for c in range(2):
            for j in range(half):
                pl.when(has_next)(z_copy[c][j].wait_send)
                pl.when(send_b)(b_copy[c][j].wait_send)
        for j in range(half):
            p_copy[j].wait_send()

    for k in range(nt - 1):
        n_copy[k].wait_recv()
        sums = sums + sq_in[k]
    inv = lax.rsqrt(sums * (1.0 / (nt * heads * HD)) + EPS)

    def as_column(r):
        return jnp.broadcast_to(r, (HD, tokens)).T

    lin_inv, att_inv = as_column(inv[0:1]), as_column(inv[1:2])
    gl, ga = gain_lin[...].astype(F32), gain_att[...].astype(F32)
    for h in range(heads):
        hs = pl.ds(h * HD, HD)
        out[:, hs] = (
            lin_out[:, hs] * lin_inv * gl[h:h + 1] + att_out[:, hs] * att_inv * ga[h:h + 1]
        ).astype(BF16)
    for c in n_copy:
        c.wait_send()


def per_device(n, nt, lin_q, lin_k, lin_v, att_q, att_k, att_v, block_lists, gain_lin, gain_att):
    tokens, columns = lin_q.shape
    heads, half = columns // HD, columns // HD // 2
    gain_lin, gain_att = gain_lin.reshape(heads, HD), gain_att.reshape(heads, HD)
    anywhere = pl.BlockSpec(memory_space=pl.ANY)
    wide, kv_wide = (tokens, columns), att_k.shape
    state, kv_heads = (half, HD, HD), kv_wide[1] // HD
    dma = pltpu.SemaphoreType.DMA
    return pl.pallas_call(
        functools.partial(kernel, n, nt),
        out_shape=pltpu.VMEM(wide, BF16),
        in_specs=[pl.BlockSpec(memory_space=pltpu.SMEM)] + [anywhere] * 8,
        out_specs=pl.BlockSpec(memory_space=pltpu.VMEM),
        scratch_shapes=[
            pltpu.VMEM(wide, BF16), pltpu.VMEM(wide, BF16), pltpu.VMEM(wide, BF16),
            pltpu.VMEM(wide, BF16), pltpu.VMEM(kv_wide, BF16), pltpu.VMEM(kv_wide, BF16),
            pltpu.VMEM((heads, HD), BF16), pltpu.VMEM((heads, HD), BF16),
            pltpu.VMEM((2, 2) + kv_wide, BF16),
            pltpu.VMEM((2,) + state, F32), pltpu.VMEM(state, F32), pltpu.VMEM((heads, HD, HD), F32),
            pltpu.VMEM(wide, BF16), pltpu.VMEM(wide, F32), pltpu.VMEM(wide, F32),
            pltpu.VMEM(state, BF16), pltpu.VMEM((2,) + state, BF16),
            pltpu.VMEM((2,) + state, BF16), pltpu.VMEM((2,) + state, BF16),
            pltpu.VMEM((2,) + state, BF16), pltpu.VMEM(state, BF16), pltpu.VMEM(state, F32),
            pltpu.VMEM((2, tokens, HD), F32),
            pltpu.VMEM((8, tokens), F32), pltpu.VMEM((nt - 1, 8, tokens), F32),
            dma((8,)), dma((2, 5)), dma((2, 5)),
            dma((half,)), dma((half,)),
            dma((half,)), dma((2, half)), dma((2, half)), dma((2, half)),
            dma((2, half)), dma((half,)), dma((half,)), dma((half,)),
            dma((nt - 1,)), dma((nt - 1,)),
        ],
        compiler_params=pltpu.CompilerParams(
            collective_id=0, has_side_effects=True, vmem_limit_bytes=63 * 2 ** 20
        ),
    )(block_lists, lin_q, lin_k, lin_v, att_q, att_k, att_v, gain_lin, gain_att)


def solution(mesh):
    wide = P("ctx", "tp")
    return jax.shard_map(
        functools.partial(per_device, mesh.shape["ctx"], mesh.shape["tp"]),
        mesh=mesh,
        in_specs=(wide,) * 6 + (P("ctx", None), P("tp"), P("tp")),
        out_specs=wide,
        check_vma=False,
    )
```

```python
import functools
import math

import jax
import jax.numpy as jnp
from jax import lax
from jax.experimental import pallas as pl
from jax.experimental.pallas import tpu as pltpu
from jax.sharding import PartitionSpec as P

HD = 128
BLK = 128
SPAN = 5
EPS = 1e-06
NEG = -1e30
MESH = pl.DeviceIdType.MESH
BF16, F32 = jnp.bfloat16, jnp.float32


def dot(a, b, dims):
    return lax.dot_general(a, b, (dims, ((), ())), preferred_element_type=F32)


def kernel(
    n, nt, lists, lin_q_h, lin_k_h, lin_v_h, att_q_h, att_k_h, att_v_h, gain_lin_h, gain_att_h,
    out, lin_q, lin_k, lin_v, att_q, att_k, att_v, gain_lin, gain_att, kv, home, pre, first, scores, lin_out, att_out,
    xout, xin, zout, zin, bout, bin_, pback, squares, sq_out, sq_in,
    lsem, kvs, kvr, hs_, hr, xs, xr, zs, zr, bs, br, ps, pr, ns, nr,
):
    ctx, tp = lax.axis_index("ctx"), lax.axis_index("tp")
    p, o = lax.rem(ctx, 2), lax.div(ctx, 2)
    core = lax.rem(tp, 2)
    chief, left = tp + 1 - core, tp - core
    lead = core == 1
    mate = ctx + 1 - 2 * p
    tokens = lin_q.shape[0]
    heads = lin_q.shape[1] // HD
    kv_heads = att_k.shape[1] // HD
    half = heads // 2
    has_prev, has_next = o > 0, o < n // 2 - 1
    side, ahead, behind = {"ctx": mate}, {"ctx": ctx + 2}, {"ctx": ctx - 2}

    pairs = (
        (lin_k_h, lin_k), (lin_v_h, lin_v), (lin_q_h, lin_q),
        (att_q_h, att_q), (att_k_h, att_k), (att_v_h, att_v),
        (gain_lin_h, gain_lin), (gain_att_h, gain_att),
    )
    local = [pltpu.make_async_copy(s, d, lsem.at[i]) for i, (s, d) in enumerate(pairs)]
    barrier = pltpu.get_barrier_semaphore()

    def greet(where):
        pl.semaphore_signal(barrier, inc=1, device_id=where, device_id_type=MESH)

    greet({"ctx": mate, "tp": left})
    greet({"ctx": mate, "tp": chief})
    pl.when(has_prev)(lambda: greet(behind))
    pl.when(has_next)(lambda: greet(ahead))
    for k in range(1, nt):
        greet({"tp": lax.rem(tp + k, nt)})
    for c in local:
        c.start()

    def remote(src, dst, ssem, rsem, where):
        return pltpu.make_async_remote_copy(
            src_ref=src, dst_ref=dst, send_sem=ssem, recv_sem=rsem,
            device_id=where, device_id_type=MESH,
        )

    pieces = [(0, 0, 0, tokens), (0, 1, 0, tokens), (1, 0, 0, tokens), (1, 1, 0, tokens // 2), (1, 1, tokens // 2, tokens // 2)]

    def kv_copies(src, slot, sem, where):
        return [
            remote(
                src[a].at[pl.ds(r, m), pl.ds(g * HD, HD)], kv.at[slot, a, pl.ds(r, m), pl.ds(g * HD, HD)],
                kvs.at[sem, i], kvr.at[sem, i], where,
            )
            for i, (g, a, r, m) in enumerate(pieces)
        ]

    kv_src = (att_k_h, att_v_h)
    kv_ahead = kv_copies(kv_src, 1, 1, ahead)
    kv_side = kv_copies(kv_src, 0, 0, side)
    kv_pass = kv_copies((kv.at[1, 0], kv.at[1, 1]), 0, 0, side)
    which = range(len(pieces))

    def send_ahead(ids):
        for i in ids:
            pl.when(has_next)(kv_ahead[i].start)

    def send_side(ids):
        for i in ids:
            pl.when(p == 0)(kv_side[i].start)

    def lanes(h):
        return pl.ds(pl.multiple_of(h * HD, HD), HD)

    x_copy = [
        remote(xout.at[j], xin.at[core, j], xs.at[j], xr.at[core, j], {"ctx": mate, "tp": chief})
        for j in range(half)
    ]
    x_recv = [
        [remote(xout.at[j], xin.at[c, j], xs.at[j], xr.at[c, j], side) for j in range(half)]
        for c in range(2)
    ]
    h_copy = [
        remote(home.at[0, j], home.at[0, j], hs_.at[j], hr.at[j], {"tp": chief})
        for j in range(half)
    ]
    z_copy = [
        [remote(zout.at[c, j], zin.at[c, j], zs.at[c, j], zr.at[c, j], ahead) for j in range(half)]
        for c in range(2)
    ]
    b_copy = [
        [
            remote(bout.at[c, j], bin_.at[j], bs.at[c, j], br.at[j], {"ctx": mate, "tp": left + c})
            for j in range(half)
        ]
        for c in range(2)
    ]
    p_copy = [
        remote(pback.at[j], pre.at[j], ps.at[j], pr.at[j], {"tp": left}) for j in range(half)
    ]
    other, mine = (1 - p) * half, p * half

    local[0].wait()
    local[1].wait()
    for j in range(half):
        h = other + j
        xout[j] = dot(lin_k[:, lanes(h)], lin_v[:, lanes(h)], ((0,), (0,))).astype(BF16)
    for j in range(half):
        h = mine + j
        home[core, j] = dot(lin_k[:, lanes(h)], lin_v[:, lanes(h)], ((0,), (0,)))

    @pl.when(jnp.logical_not(has_prev))
    def _():
        kv[1] = jnp.zeros_like(kv[1])

        @pl.when(p == 0)
        def _():
            kv[0] = jnp.zeros_like(kv[0])
            bin_[...] = jnp.zeros_like(bin_)

    pl.semaphore_wait(barrier, nt + 1 + has_prev.astype(jnp.int32) + has_next.astype(jnp.int32))

    send_x = (p == 0) | has_next
    take_x = (p == 1) | has_next
    send_b = (p == 0) | has_prev
    take_b = (p == 1) | has_prev

    def start_x():
        for j in range(half):
            x_copy[j].start()

    @pl.when(jnp.logical_not(lead))
    def _():
        for j in range(half):
            h_copy[j].start()

    rest = which[2:]
    pl.when(send_x & (o < 2))(start_x)
    send_ahead((0,))
    pl.when((o > 0) | jnp.logical_not(lead))(lambda: send_ahead((1,)))
    send_side((0, 1))
    pl.when((o > 0) | jnp.logical_not(lead))(lambda: send_ahead((2,)))
    pl.when((o > 1) | (o == 1) & (jnp.logical_not(lead) | (p == 1)))(lambda: send_ahead((3, 4)))
    pl.when(send_x & (o >= 2) & has_next)(start_x)
    send_side(rest)
    pl.when(send_x & (o >= 2) & jnp.logical_not(has_next))(start_x)

    local[2].wait()
    row = lax.broadcasted_iota(jnp.int32, (BLK, BLK), 0)
    col = lax.broadcasted_iota(jnp.int32, (BLK, BLK), 1)
    lower = row >= col
    blocks = tokens // BLK
    for h in range(heads):
        hs = pl.ds(h * HD, HD)
        for b in range(blocks):
            rows = pl.ds(b * BLK, BLK)
            s = dot(lin_q[rows, hs], lin_k[rows, hs], ((1,), (1,)))
            scores[rows, hs] = jnp.where(lower, s, 0.0).astype(BF16)
        first[h] = dot(lin_k[0:BLK, hs], lin_v[0:BLK, hs], ((0,), (0,)))

    def forward(ids):
        @pl.when(has_prev)
        def _():
            for i in ids:
                kv_ahead[i].wait_recv()
                pl.when(p == 1)(kv_pass[i].start)

    def finish(h, prefix, fresh):
        for b in range(blocks):
            rows = pl.ds(b * BLK, BLK)
            low = (prefix if b == 0 else prefix + first[h]).astype(BF16)
            lhs = jnp.concatenate([scores[rows, lanes(h)], lin_q[rows, lanes(h)]], axis=1)
            rhs = jnp.concatenate([lin_v[rows, lanes(h)], low], axis=0)
            r = dot(lhs, rhs, ((1,), (0,)))
            lin_out[rows, lanes(h)] = r
            squares[0, rows] = r * r if fresh else squares[0, rows] + r * r

    def link(c, j):
        @pl.when(has_prev)
        def _():
            z_copy[c][j].wait_recv()

        @pl.when(jnp.logical_not(has_prev))
        def _():
            zin[c, j] = jnp.zeros_like(zin[c, j])

        if c == 0:
            h_copy[j].wait_recv()
        before, here = zin[c, j].astype(F32), home[c, j]
        @pl.when(has_next)
        def _():
            x_recv[c][j].wait_recv()
            zout[c, j] = (before + here + xin[c, j].astype(F32)).astype(BF16)
            z_copy[c][j].start()
        bout[c, j] = jnp.where(p == 0, before + here, before).astype(BF16)
        pl.when(send_b)(b_copy[c][j].start)
        back = pback if c == 0 else pre

        @pl.when(p == 0)
        def _():
            back[j] = before

        @pl.when(p == 1)
        def _():
            pl.when(jnp.logical_not(has_next))(x_recv[c][j].wait_recv)
            back[j] = before + xin[c, j].astype(F32)

        if c == 0:
            p_copy[j].start()
        else:
            finish(mine + j, pre[j], j == 0)

    quarter = half // 2
    steps = [(1, j) for j in range(quarter)] + [(0, j) for j in range(half)] + [(1, j) for j in range(quarter, half)]

    def chain():
        for c, j in steps:
            link(c, j)

    def weave(at=()):
        for k, (c, j) in enumerate(steps):
            forward([i for i, step in at if step == k])
            link(c, j)

    inner = lead & has_prev & has_next
    final = lead & has_prev & jnp.logical_not(has_next)
    woven = inner & (o >= 2) & (p == 1)

    @pl.when(lead & jnp.logical_not(has_prev))
    def _():
        chain()
        send_ahead((1, 2, 3, 4))

    def late_kv():
        for j in range(half):
            p_copy[j].wait_recv()
        send_ahead((3, 4))

    for c in local[3:]:
        c.wait()
    factor = (HD ** -0.5) * math.log2(math.e)
    bias = []
    for b in range(blocks):
        parts = []
        for i in range(SPAN - 1):
            key_block = ctx * blocks + b - (SPAN - 1) + i
            hit = lists[b, 0] == key_block
            for e in range(1, 4):
                hit = hit | (lists[b, e] == key_block)
            value = jnp.where(hit & (key_block >= 0), 0.0, NEG).astype(F32)
            parts.append(jnp.full((1, BLK), value, F32))
        bias.append(parts)

    kept, weights, scales = {}, {}, {}

    def group_of(g):
        return range(g * heads // kv_heads, (g + 1) * heads // kv_heads)

    def queries_of(g, b):
        rows = pl.ds(b * BLK, BLK)
        return jnp.concatenate([att_q[rows, pl.ds(h * HD, HD)] for h in group_of(g)], axis=0)

    def window(g, b, a, own):
        gs = pl.ds(g * HD, HD)
        return jnp.concatenate([kv[1, a, b * BLK:, gs], own[: (b + 1) * BLK, gs]], axis=0)

    def weigh_near(g):
        for b in range(blocks):
            keys = window(g, b, 0, att_k)
            sall = dot(queries_of(g, b), keys, ((1,), (1,)))
            cut = sall.shape[1] - BLK
            add = jnp.concatenate(bias[b][: blocks - b] + bias[b][2 * blocks - b:], axis=1)
            wall = []
            for i in range(len(group_of(g))):
                s = sall[i * BLK:(i + 1) * BLK]
                s = jnp.concatenate([s[:, :cut] + add, jnp.where(lower, s[:, cut:], NEG)], axis=1)
                m = jnp.max(s, axis=1, keepdims=True)
                e = jnp.exp2((s - m) * factor)
                kept[g, b, i] = (m, jnp.sum(e, axis=1, keepdims=True))
                wall.append(e.astype(BF16))
            weights[g, b] = jnp.concatenate(wall, axis=0)

    def sum_near(g):
        for b in range(blocks):
            rows = pl.ds(b * BLK, BLK)
            rall = dot(weights.pop((g, b)), window(g, b, 1, att_v), ((1,), (0,)))
            for i, h in enumerate(group_of(g)):
                att_out[rows, pl.ds(h * HD, HD)] = rall[i * BLK:(i + 1) * BLK]

    def await_far(g, which_of):
        for i in which:
            if pieces[i][:2] == (g, which_of):
                pl.when((p == 1) | has_prev)(kv_side[i].wait_recv)

    def weigh_far(g):
        gs = pl.ds(g * HD, HD)
        await_far(g, 0)
        for b in range(blocks):
            sall = dot(queries_of(g, b), kv[0, 0, :, gs], ((1,), (1,)))
            add = jnp.concatenate(bias[b][blocks - b: 2 * blocks - b], axis=1)
            wall, scale = [], []
            scales[g, b] = scale
            for i in range(len(group_of(g))):
                m_near, l_near = kept[g, b, i]
                s = sall[i * BLK:(i + 1) * BLK] + add
                m = jnp.maximum(m_near, jnp.max(s, axis=1, keepdims=True))
                e = jnp.exp2((s - m) * factor)
                keep = jnp.exp2((m_near - m) * factor)
                inv = 1.0 / (keep * l_near + jnp.sum(e, axis=1, keepdims=True))
                scale.append((keep * inv, inv))
                wall.append(e.astype(BF16))
            weights[g, b] = jnp.concatenate(wall, axis=0)

    def sum_far(g):
        gs = pl.ds(g * HD, HD)
        await_far(g, 1)
        for b in range(blocks):
            rows, scale = pl.ds(b * BLK, BLK), scales[g, b]
            rall = dot(weights[g, b], kv[0, 1, :, gs], ((1,), (0,)))
            sq = None if g == 0 else squares[1, rows]
            for i, h in enumerate(group_of(g)):
                hs = pl.ds(h * HD, HD)
                r = att_out[rows, hs] * scale[i][0] + rall[i * BLK:(i + 1) * BLK] * scale[i][1]
                att_out[rows, hs] = r
                sq = r * r if sq is None else sq + r * r
            squares[1, rows] = sq

    def finish_mine():
        for j in range(half):
            pl.when(o > 0)(p_copy[j].wait_recv)
            finish(mine + j, pre[j], j == 0)

    def far_first():
        weigh_far(0)
        sum_far(0)

    def finish_other():
        for j in range(half):
            pl.when(take_b)(b_copy[0][j].wait_recv)
            finish(other + j, bin_[j].astype(F32), False)

    deep = inner & (o >= 2)
    far_soon = (o >= 2) & (p == 1) & lead
    forward((0,))
    weigh_near(0)
    pl.when(inner & (o < 2))(weave)
    pl.when(inner & (o == 1) & (p == 0))(lambda: send_ahead((3, 4)))
    forward((1,))
    sum_near(0)
    pl.when(far_soon)(far_first)
    pl.when(jnp.logical_not(lead) & (o == 0))(late_kv)
    pl.when(jnp.logical_not(lead) & (o == 0))(finish_mine)
    forward((2,))
    weigh_near(1)
    pl.when(woven)(lambda: weave(((3, 2), (4, 4))))
    pl.when(deep & (p == 0))(weave)
    pl.when(jnp.logical_not(far_soon))(far_first)
    pl.when(jnp.logical_not(woven))(lambda: forward((3, 4)))
    sum_near(1)
    pl.when(final & (p == 0))(chain)
    weigh_far(1)
    pl.when(final & (p == 1))(chain)
    pl.when(jnp.logical_not(lead) & (o > 0))(finish_mine)
    pl.when(has_next)(finish_other)
    sum_far(1)
    pl.when(jnp.logical_not(has_next))(finish_other)

    def as_row(sq):
        return jnp.sum(sq.T, axis=0, keepdims=True)

    top = lax.broadcasted_iota(jnp.int32, (8, tokens), 0) == 0
    sums = jnp.where(top, as_row(squares[0]), as_row(squares[1]))
    sq_out[...] = sums
    n_copy = [
        remote(sq_out, sq_in.at[k - 1], ns.at[k - 1], nr.at[k - 1], {"tp": lax.rem(tp + k, nt)})
        for k in range(1, nt)
    ]
    for c in n_copy:
        c.start()
    for i in which:
        pl.when(has_next)(kv_ahead[i].wait_send)
        pl.when(p == 0)(kv_side[i].wait_send)

    @pl.when((p == 1) & has_prev)
    def _():
        for i in which:
            kv_pass[i].wait_send()

    for j in range(half):
        pl.when(send_x)(x_copy[j].wait_send)
        pl.when(jnp.logical_not(lead))(h_copy[j].wait_send)

    @pl.when(lead)
    def _():
        for c in range(2):
            for j in range(half):
                pl.when(has_next)(z_copy[c][j].wait_send)
                pl.when(send_b)(b_copy[c][j].wait_send)
        for j in range(half):
            p_copy[j].wait_send()

    for k in range(nt - 1):
        n_copy[k].wait_recv()
        sums = sums + sq_in[k]
    inv = lax.rsqrt(sums * (1.0 / (nt * heads * HD)) + EPS)

    def as_column(r):
        return jnp.broadcast_to(r, (HD, tokens)).T

    lin_inv, att_inv = as_column(inv[0:1]), as_column(inv[1:2])
    gl, ga = gain_lin[...].astype(F32), gain_att[...].astype(F32)
    for h in range(heads):
        hs = pl.ds(h * HD, HD)
        out[:, hs] = (
            lin_out[:, hs] * lin_inv * gl[h:h + 1] + att_out[:, hs] * att_inv * ga[h:h + 1]
        ).astype(BF16)
    for c in n_copy:
        c.wait_send()


def per_device(n, nt, lin_q, lin_k, lin_v, att_q, att_k, att_v, block_lists, gain_lin, gain_att):
    tokens, columns = lin_q.shape
    heads, half = columns // HD, columns // HD // 2
    gain_lin, gain_att = gain_lin.reshape(heads, HD), gain_att.reshape(heads, HD)
    anywhere = pl.BlockSpec(memory_space=pl.ANY)
    wide, kv_wide = (tokens, columns), att_k.shape
    state, kv_heads = (half, HD, HD), kv_wide[1] // HD
    dma = pltpu.SemaphoreType.DMA
    return pl.pallas_call(
        functools.partial(kernel, n, nt),
        out_shape=pltpu.VMEM(wide, BF16),
        in_specs=[pl.BlockSpec(memory_space=pltpu.SMEM)] + [anywhere] * 8,
        out_specs=pl.BlockSpec(memory_space=pltpu.VMEM),
        scratch_shapes=[
            pltpu.VMEM(wide, BF16), pltpu.VMEM(wide, BF16), pltpu.VMEM(wide, BF16),
            pltpu.VMEM(wide, BF16), pltpu.VMEM(kv_wide, BF16), pltpu.VMEM(kv_wide, BF16),
            pltpu.VMEM((heads, HD), BF16), pltpu.VMEM((heads, HD), BF16),
            pltpu.VMEM((2, 2) + kv_wide, BF16),
            pltpu.VMEM((2,) + state, F32), pltpu.VMEM(state, F32), pltpu.VMEM((heads, HD, HD), F32),
            pltpu.VMEM(wide, BF16), pltpu.VMEM(wide, F32), pltpu.VMEM(wide, F32),
            pltpu.VMEM(state, BF16), pltpu.VMEM((2,) + state, BF16),
            pltpu.VMEM((2,) + state, BF16), pltpu.VMEM((2,) + state, BF16),
            pltpu.VMEM((2,) + state, BF16), pltpu.VMEM(state, BF16), pltpu.VMEM(state, F32),
            pltpu.VMEM((2, tokens, HD), F32),
            pltpu.VMEM((8, tokens), F32), pltpu.VMEM((nt - 1, 8, tokens), F32),
            dma((8,)), dma((2, 5)), dma((2, 5)),
            dma((half,)), dma((half,)),
            dma((half,)), dma((2, half)), dma((2, half)), dma((2, half)),
            dma((2, half)), dma((half,)), dma((half,)), dma((half,)),
            dma((nt - 1,)), dma((nt - 1,)),
        ],
        compiler_params=pltpu.CompilerParams(
            collective_id=0, has_side_effects=True, vmem_limit_bytes=63 * 2 ** 20
        ),
    )(block_lists, lin_q, lin_k, lin_v, att_q, att_k, att_v, gain_lin, gain_att)


def solution(mesh):
    wide = P("ctx", "tp")
    return jax.shard_map(
        functools.partial(per_device, mesh.shape["ctx"], mesh.shape["tp"]),
        mesh=mesh,
        in_specs=(wide,) * 6 + (P("ctx", None), P("tp"), P("tp")),
        out_specs=wide,
        check_vma=False,
    )
```

```python
import functools
import math

import jax
import jax.numpy as jnp
from jax import lax
from jax.experimental import pallas as pl
from jax.experimental.pallas import tpu as pltpu
from jax.sharding import PartitionSpec as P

HD = 128
BLK = 128
SPAN = 5
EPS = 1e-06
NEG = -1e30
MESH = pl.DeviceIdType.MESH
BF16, F32 = jnp.bfloat16, jnp.float32


def dot(a, b, dims):
    return lax.dot_general(a, b, (dims, ((), ())), preferred_element_type=F32)


def kernel(
    n, nt, lists, lin_q_h, lin_k_h, lin_v_h, att_q_h, att_k_h, att_v_h, gain_lin_h, gain_att_h,
    lin_out, att_out, inverse, lin_q, lin_k, lin_v, att_q, att_k, att_v, gain_lin, gain_att, wide_gains, kv, home, pre, first, scores,
    xout, xin, zout, zin, bout, bin_, pback, squares, sq_out, sq_in,
    lsem, kvs, kvr, hs_, hr, xs, xr, zs, zr, bs, br, ps, pr, ns, nr,
):
    ctx, tp = lax.axis_index("ctx"), lax.axis_index("tp")
    p, o = lax.rem(ctx, 2), lax.div(ctx, 2)
    core = lax.rem(tp, 2)
    chief, left = tp + 1 - core, tp - core
    lead = core == 1
    mate = ctx + 1 - 2 * p
    tokens = lin_q.shape[0]
    heads = lin_q.shape[1] // HD
    kv_heads = att_k.shape[1] // HD
    half = heads // 2
    has_prev, has_next = o > 0, o < n // 2 - 1
    side, ahead, behind = {"ctx": mate}, {"ctx": ctx + 2}, {"ctx": ctx - 2}

    other, mine = (1 - p) * half, p * half

    def columns(ref, h):
        return ref.at[:, pl.ds(pl.multiple_of(h * HD, HD), half * HD)]

    pairs = (
        (columns(lin_k_h, other), columns(lin_k, other)), (columns(lin_v_h, other), columns(lin_v, other)),
        (columns(lin_k_h, mine), columns(lin_k, mine)), (columns(lin_v_h, mine), columns(lin_v, mine)),
        (lin_q_h, lin_q),
        (gain_lin_h, gain_lin), (gain_att_h, gain_att),
        (att_q_h, att_q), (att_k_h, att_k), (att_v_h, att_v),
    )
    local = [pltpu.make_async_copy(s, d, lsem.at[i]) for i, (s, d) in enumerate(pairs)]
    barrier = pltpu.get_barrier_semaphore()

    def greet(where):
        pl.semaphore_signal(barrier, inc=1, device_id=where, device_id_type=MESH)

    greet({"ctx": mate, "tp": left})
    greet({"ctx": mate, "tp": chief})
    pl.when(has_prev)(lambda: greet(behind))
    pl.when(has_next)(lambda: greet(ahead))
    for k in range(1, nt):
        greet({"tp": lax.rem(tp + k, nt)})
    for c in local:
        c.start()

    def remote(src, dst, ssem, rsem, where):
        return pltpu.make_async_remote_copy(
            src_ref=src, dst_ref=dst, send_sem=ssem, recv_sem=rsem,
            device_id=where, device_id_type=MESH,
        )

    pieces = [(0, 0, 0, tokens), (0, 1, 0, tokens), (1, 0, 0, tokens), (1, 1, 0, tokens // 2), (1, 1, tokens // 2, tokens // 2)]

    def kv_copies(src, slot, sem, where):
        return [
            remote(
                src[a].at[pl.ds(r, m), pl.ds(g * HD, HD)], kv.at[slot, a, pl.ds(r, m), pl.ds(g * HD, HD)],
                kvs.at[sem, i], kvr.at[sem, i], where,
            )
            for i, (g, a, r, m) in enumerate(pieces)
        ]

    kv_src = (att_k_h, att_v_h)
    kv_ahead = kv_copies(kv_src, 1, 1, ahead)
    kv_side = kv_copies(kv_src, 0, 0, side)
    kv_pass = kv_copies((kv.at[1, 0], kv.at[1, 1]), 0, 0, side)
    which = range(len(pieces))

    def send_ahead(ids):
        for i in ids:
            pl.when(has_next)(kv_ahead[i].start)

    def send_side(ids):
        for i in ids:
            pl.when(p == 0)(kv_side[i].start)

    def lanes(h):
        return pl.ds(pl.multiple_of(h * HD, HD), HD)

    x_copy = [
        remote(xout.at[j], xin.at[core, j], xs.at[j], xr.at[core, j], {"ctx": mate, "tp": chief})
        for j in range(half)
    ]
    x_recv = [
        [remote(xout.at[j], xin.at[c, j], xs.at[j], xr.at[c, j], side) for j in range(half)]
        for c in range(2)
    ]
    h_copy = [
        remote(home.at[0, j], home.at[0, j], hs_.at[j], hr.at[j], {"tp": chief})
        for j in range(half)
    ]
    z_copy = [
        [remote(zout.at[c, j], zin.at[c, j], zs.at[c, j], zr.at[c, j], ahead) for j in range(half)]
        for c in range(2)
    ]
    b_copy = [
        [
            remote(bout.at[c, j], bin_.at[j], bs.at[c, j], br.at[j], {"ctx": mate, "tp": left + c})
            for j in range(half)
        ]
        for c in range(2)
    ]
    p_copy = [
        remote(pback.at[j], pre.at[j], ps.at[j], pr.at[j], {"tp": left}) for j in range(half)
    ]
    local[0].wait()
    local[1].wait()
    for j in range(half):
        h = other + j
        xout[j] = dot(lin_k[:, lanes(h)], lin_v[:, lanes(h)], ((0,), (0,))).astype(BF16)
    @pl.when(jnp.logical_not(has_prev))
    def _():
        kv[1] = jnp.zeros_like(kv[1])

        @pl.when(p == 0)
        def _():
            kv[0] = jnp.zeros_like(kv[0])
            bin_[...] = jnp.zeros_like(bin_)

    pl.semaphore_wait(barrier, nt + 1 + has_prev.astype(jnp.int32) + has_next.astype(jnp.int32))

    send_x = (p == 0) | has_next
    take_x = (p == 1) | has_next
    send_b = (p == 0) | has_prev
    take_b = (p == 1) | has_prev

    def start_x(first_head=0, end=half):
        for j in range(first_head, end):
            x_copy[j].start()

    rest = which[2:]
    yields = lead & (o < 2)
    pl.when(send_x & (o < 2))(lambda: start_x(0, half // 2))
    pl.when(send_x & (o < 2) & jnp.logical_not(lead))(lambda: start_x(half // 2))
    send_ahead((0,))
    pl.when((o > 0) | jnp.logical_not(lead))(lambda: send_ahead((1,)))
    pl.when(jnp.logical_not(yields))(lambda: send_side((0, 1)))
    pl.when((o > 0) | jnp.logical_not(lead))(lambda: send_ahead((2,)))
    pl.when((o > 1) | (o == 1) & (jnp.logical_not(lead) | (p == 1)))(lambda: send_ahead((3, 4)))
    pl.when(send_x & (o >= 2) & has_next)(start_x)
    pl.when(jnp.logical_not(yields))(lambda: send_side(rest))
    pl.when(send_x & (o >= 2) & jnp.logical_not(has_next))(start_x)

    local[2].wait()
    local[3].wait()
    for j in range(half):
        h = mine + j
        home[core, j] = dot(lin_k[:, lanes(h)], lin_v[:, lanes(h)], ((0,), (0,)))

    @pl.when(jnp.logical_not(lead))
    def _():
        for j in range(half):
            h_copy[j].start()

    @pl.when(yields)
    def _():
        pl.when(send_x)(lambda: start_x(half // 2))
        send_side(which)


    for c in local[4:7]:
        c.wait()
    wide_gains[0] = gain_lin[...].astype(F32)
    wide_gains[1] = gain_att[...].astype(F32)
    row = lax.broadcasted_iota(jnp.int32, (BLK, BLK), 0)
    col = lax.broadcasted_iota(jnp.int32, (BLK, BLK), 1)
    lower = row >= col
    blocks = tokens // BLK
    for h in range(heads):
        hs = pl.ds(h * HD, HD)
        for b in range(blocks):
            rows = pl.ds(b * BLK, BLK)
            s = dot(lin_q[rows, hs], lin_k[rows, hs], ((1,), (1,)))
            scores[rows, hs] = jnp.where(lower, s, 0.0).astype(BF16)
        first[h] = dot(lin_k[0:BLK, hs], lin_v[0:BLK, hs], ((0,), (0,)))

    def forward(ids):
        @pl.when(has_prev)
        def _():
            for i in ids:
                kv_ahead[i].wait_recv()
                pl.when(p == 1)(kv_pass[i].start)

    def finish(h, prefix, fresh):
        for b in range(blocks):
            rows = pl.ds(b * BLK, BLK)
            low = (prefix if b == 0 else prefix + first[h]).astype(BF16)
            lhs = jnp.concatenate([scores[rows, lanes(h)], lin_q[rows, lanes(h)]], axis=1)
            rhs = jnp.concatenate([lin_v[rows, lanes(h)], low], axis=0)
            r = dot(lhs, rhs, ((1,), (0,)))
            lin_out[rows, lanes(h)] = r * wide_gains[0, pl.ds(h, 1)]
            squares[0, rows] = r * r if fresh else squares[0, rows] + r * r

    def link(c, j):
        @pl.when(has_prev)
        def _():
            z_copy[c][j].wait_recv()

        @pl.when(jnp.logical_not(has_prev))
        def _():
            zin[c, j] = jnp.zeros_like(zin[c, j])

        if c == 0:
            h_copy[j].wait_recv()
        before, here = zin[c, j].astype(F32), home[c, j]
        @pl.when(has_next)
        def _():
            x_recv[c][j].wait_recv()
            zout[c, j] = (before + here + xin[c, j].astype(F32)).astype(BF16)
            z_copy[c][j].start()
        bout[c, j] = jnp.where(p == 0, before + here, before).astype(BF16)
        pl.when(send_b)(b_copy[c][j].start)
        back = pback if c == 0 else pre

        @pl.when(p == 0)
        def _():
            back[j] = before

        @pl.when(p == 1)
        def _():
            pl.when(jnp.logical_not(has_next))(x_recv[c][j].wait_recv)
            back[j] = before + xin[c, j].astype(F32)

        if c == 0:
            p_copy[j].start()
        else:
            finish(mine + j, pre[j], j == 0)

    quarter = half // 2
    steps = [(1, j) for j in range(quarter)] + [(0, j) for j in range(half)] + [(1, j) for j in range(quarter, half)]

    def chain():
        for c, j in steps:
            link(c, j)

    def weave(at=()):
        for k, (c, j) in enumerate(steps):
            forward([i for i, step in at if step == k])
            link(c, j)

    inner = lead & has_prev & has_next
    final = lead & has_prev & jnp.logical_not(has_next)
    woven = inner & (o >= 2) & (p == 1)

    @pl.when(lead & jnp.logical_not(has_prev))
    def _():
        chain()
        send_ahead((1, 2, 3, 4))

    def late_kv():
        for j in range(half):
            p_copy[j].wait_recv()
        send_ahead((3, 4))

    for c in local[7:]:
        c.wait()
    factor = (HD ** -0.5) * math.log2(math.e)
    bias = []
    for b in range(blocks):
        parts = []
        for i in range(SPAN - 1):
            key_block = ctx * blocks + b - (SPAN - 1) + i
            hit = lists[b, 0] == key_block
            for e in range(1, 4):
                hit = hit | (lists[b, e] == key_block)
            value = jnp.where(hit & (key_block >= 0), 0.0, NEG).astype(F32)
            parts.append(jnp.full((1, BLK), value, F32))
        bias.append(parts)

    kept, weights, scales = {}, {}, {}

    def group_of(g):
        return range(g * heads // kv_heads, (g + 1) * heads // kv_heads)

    def queries_of(g, b):
        rows = pl.ds(b * BLK, BLK)
        return jnp.concatenate([att_q[rows, pl.ds(h * HD, HD)] for h in group_of(g)], axis=0)

    def window(g, b, a, own):
        gs = pl.ds(g * HD, HD)
        return jnp.concatenate([kv[1, a, b * BLK:, gs], own[: (b + 1) * BLK, gs]], axis=0)

    def weigh_near(g):
        for b in range(blocks):
            keys = window(g, b, 0, att_k)
            sall = dot(queries_of(g, b), keys, ((1,), (1,)))
            cut = sall.shape[1] - BLK
            add = jnp.concatenate(bias[b][: blocks - b] + bias[b][2 * blocks - b:], axis=1)
            wall = []
            for i in range(len(group_of(g))):
                s = sall[i * BLK:(i + 1) * BLK]
                s = jnp.concatenate([s[:, :cut] + add, jnp.where(lower, s[:, cut:], NEG)], axis=1)
                m = jnp.max(s, axis=1, keepdims=True)
                e = jnp.exp2((s - m) * factor)
                kept[g, b, i] = (m, jnp.sum(e, axis=1, keepdims=True))
                wall.append(e.astype(BF16))
            weights[g, b] = jnp.concatenate(wall, axis=0)

    def sum_near(g):
        for b in range(blocks):
            rows = pl.ds(b * BLK, BLK)
            rall = dot(weights.pop((g, b)), window(g, b, 1, att_v), ((1,), (0,)))
            for i, h in enumerate(group_of(g)):
                att_out[rows, pl.ds(h * HD, HD)] = rall[i * BLK:(i + 1) * BLK]

    def await_far(g, which_of):
        for i in which:
            if pieces[i][:2] == (g, which_of):
                pl.when((p == 1) | has_prev)(kv_side[i].wait_recv)

    def weigh_far(g):
        gs = pl.ds(g * HD, HD)
        await_far(g, 0)
        for b in range(blocks):
            sall = dot(queries_of(g, b), kv[0, 0, :, gs], ((1,), (1,)))
            add = jnp.concatenate(bias[b][blocks - b: 2 * blocks - b], axis=1)
            wall, scale = [], []
            scales[g, b] = scale
            for i in range(len(group_of(g))):
                m_near, l_near = kept[g, b, i]
                s = sall[i * BLK:(i + 1) * BLK] + add
                m = jnp.maximum(m_near, jnp.max(s, axis=1, keepdims=True))
                e = jnp.exp2((s - m) * factor)
                keep = jnp.exp2((m_near - m) * factor)
                inv = 1.0 / (keep * l_near + jnp.sum(e, axis=1, keepdims=True))
                scale.append((keep * inv, inv))
                wall.append(e.astype(BF16))
            weights[g, b] = jnp.concatenate(wall, axis=0)

    def sum_far(g):
        gs = pl.ds(g * HD, HD)
        await_far(g, 1)
        for b in range(blocks):
            rows, scale = pl.ds(b * BLK, BLK), scales[g, b]
            rall = dot(weights[g, b], kv[0, 1, :, gs], ((1,), (0,)))
            sq = None if g == 0 else squares[1, rows]
            for i, h in enumerate(group_of(g)):
                hs = pl.ds(h * HD, HD)
                r = att_out[rows, hs] * scale[i][0] + rall[i * BLK:(i + 1) * BLK] * scale[i][1]
                att_out[rows, hs] = r * wide_gains[1, h:h + 1]
                sq = r * r if sq is None else sq + r * r
            squares[1, rows] = sq

    def finish_mine():
        for j in range(half):
            pl.when(o > 0)(p_copy[j].wait_recv)
            finish(mine + j, pre[j], j == 0)

    def far_first():
        weigh_far(0)
        sum_far(0)

    def finish_other():
        for j in range(half):
            pl.when(take_b)(b_copy[0][j].wait_recv)
            finish(other + j, bin_[j].astype(F32), False)

    deep = inner & (o >= 2)
    far_soon = (o >= 2) & (p == 1) & lead
    forward((0,))
    weigh_near(0)
    pl.when(inner & (o < 2))(weave)
    pl.when(inner & (o == 1) & (p == 0))(lambda: send_ahead((3, 4)))
    forward((1,))
    sum_near(0)
    pl.when(far_soon)(far_first)
    pl.when(jnp.logical_not(lead) & (o == 0))(late_kv)
    pl.when(jnp.logical_not(lead) & (o == 0))(finish_mine)
    forward((2,))
    weigh_near(1)
    pl.when(woven)(lambda: weave(((3, 2), (4, 4))))
    pl.when(deep & (p == 0))(weave)
    pl.when(jnp.logical_not(far_soon))(far_first)
    pl.when(jnp.logical_not(woven))(lambda: forward((3, 4)))
    sum_near(1)
    pl.when(final & (p == 0))(chain)
    weigh_far(1)
    pl.when(final & (p == 1))(chain)
    pl.when(jnp.logical_not(lead) & (o > 0))(finish_mine)
    pl.when(has_next)(finish_other)
    sum_far(1)
    pl.when(jnp.logical_not(has_next))(finish_other)

    def as_row(sq):
        return jnp.sum(sq.T, axis=0, keepdims=True)

    top = lax.broadcasted_iota(jnp.int32, (8, tokens), 0) == 0
    sums = jnp.where(top, as_row(squares[0]), as_row(squares[1]))
    sq_out[...] = sums
    n_copy = [
        remote(sq_out, sq_in.at[k - 1], ns.at[k - 1], nr.at[k - 1], {"tp": lax.rem(tp + k, nt)})
        for k in range(1, nt)
    ]
    for c in n_copy:
        c.start()
    for i in which:
        pl.when(has_next)(kv_ahead[i].wait_send)
        pl.when(p == 0)(kv_side[i].wait_send)

    @pl.when((p == 1) & has_prev)
    def _():
        for i in which:
            kv_pass[i].wait_send()

    for j in range(half):
        pl.when(send_x)(x_copy[j].wait_send)
        pl.when(jnp.logical_not(lead))(h_copy[j].wait_send)

    @pl.when(lead)
    def _():
        for c in range(2):
            for j in range(half):
                pl.when(has_next)(z_copy[c][j].wait_send)
                pl.when(send_b)(b_copy[c][j].wait_send)
        for j in range(half):
            p_copy[j].wait_send()

    for k in range(nt - 1):
        n_copy[k].wait_recv()
        sums = sums + sq_in[k]
    inverse[...] = lax.rsqrt(sums * (1.0 / (nt * heads * HD)) + EPS)
    for c in n_copy:
        c.wait_send()


def combine(inverse, lin_out, att_out, out_h, out, sem):
    tokens, width = out.shape

    def as_column(r):
        return jnp.broadcast_to(r, (HD, tokens)).T

    lin_inv, att_inv = as_column(inverse[0:1]), as_column(inverse[1:2])
    cuts = 4
    copies = []
    for q in range(cuts):
        m = tokens // cuts
        rows = pl.ds(q * m, m)
        li, ai = lin_inv[q * m:(q + 1) * m], att_inv[q * m:(q + 1) * m]
        for h in range(width // HD):
            hs = pl.ds(h * HD, HD)
            out[rows, hs] = (lin_out[rows, hs] * li + att_out[rows, hs] * ai).astype(BF16)
        copies.append(pltpu.make_async_copy(out.at[rows], out_h.at[rows], sem.at[q]))
        copies[-1].start()
    for c in copies:
        c.wait()


def per_device(n, nt, lin_q, lin_k, lin_v, att_q, att_k, att_v, block_lists, gain_lin, gain_att):
    tokens, columns = lin_q.shape
    heads, half = columns // HD, columns // HD // 2
    gain_lin, gain_att = gain_lin.reshape(heads, HD), gain_att.reshape(heads, HD)
    anywhere, inside = pl.BlockSpec(memory_space=pl.ANY), pl.BlockSpec(memory_space=pltpu.VMEM)
    wide, kv_wide = (tokens, columns), att_k.shape
    state, kv_heads = (half, HD, HD), kv_wide[1] // HD
    dma = pltpu.SemaphoreType.DMA
    lin_out, att_out, inverse = pl.pallas_call(
        functools.partial(kernel, n, nt),
        out_shape=(pltpu.VMEM(wide, F32), pltpu.VMEM(wide, F32), pltpu.VMEM((8, tokens), F32)),
        in_specs=[pl.BlockSpec(memory_space=pltpu.SMEM)] + [anywhere] * 8,
        out_specs=[inside] * 3,
        scratch_shapes=[
            pltpu.VMEM(wide, BF16), pltpu.VMEM(wide, BF16), pltpu.VMEM(wide, BF16),
            pltpu.VMEM(wide, BF16), pltpu.VMEM(kv_wide, BF16), pltpu.VMEM(kv_wide, BF16),
            pltpu.VMEM((heads, HD), BF16), pltpu.VMEM((heads, HD), BF16), pltpu.VMEM((2, heads, HD), F32),
            pltpu.VMEM((2, 2) + kv_wide, BF16),
            pltpu.VMEM((2,) + state, F32), pltpu.VMEM(state, F32), pltpu.VMEM((heads, HD, HD), F32),
            pltpu.VMEM(wide, BF16),
            pltpu.VMEM(state, BF16), pltpu.VMEM((2,) + state, BF16),
            pltpu.VMEM((2,) + state, BF16), pltpu.VMEM((2,) + state, BF16),
            pltpu.VMEM((2,) + state, BF16), pltpu.VMEM(state, BF16), pltpu.VMEM(state, F32),
            pltpu.VMEM((2, tokens, HD), F32),
            pltpu.VMEM((8, tokens), F32), pltpu.VMEM((nt - 1, 8, tokens), F32),
            dma((10,)), dma((2, 5)), dma((2, 5)),
            dma((half,)), dma((half,)),
            dma((half,)), dma((2, half)), dma((2, half)), dma((2, half)),
            dma((2, half)), dma((half,)), dma((half,)), dma((half,)),
            dma((nt - 1,)), dma((nt - 1,)),
        ],
        compiler_params=pltpu.CompilerParams(
            collective_id=0, has_side_effects=True, vmem_limit_bytes=62 * 2 ** 20 - 2 ** 17
        ),
    )(block_lists, lin_q, lin_k, lin_v, att_q, att_k, att_v, gain_lin, gain_att)
    return pl.pallas_call(
        combine,
        out_shape=jax.ShapeDtypeStruct(wide, BF16),
        in_specs=[inside] * 3,
        out_specs=anywhere,
        scratch_shapes=[pltpu.VMEM(wide, BF16), dma((4,))],
        compiler_params=pltpu.CompilerParams(vmem_limit_bytes=16 * 2 ** 20),
    )(inverse, lin_out, att_out)


def solution(mesh):
    wide = P("ctx", "tp")
    return jax.shard_map(
        functools.partial(per_device, mesh.shape["ctx"], mesh.shape["tp"]),
        mesh=mesh,
        in_specs=(wide,) * 6 + (P("ctx", None), P("tp"), P("tp")),
        out_specs=wide,
        check_vma=False,
    )
```

```python
import functools
import math

import jax
import jax.numpy as jnp
from jax import lax
from jax.experimental import pallas as pl
from jax.experimental.pallas import tpu as pltpu
from jax.sharding import PartitionSpec as P

HD = 128
BLK = 128
SPAN = 5
EPS = 1e-06
NEG = -1e30
MESH = pl.DeviceIdType.MESH
BF16, F32 = jnp.bfloat16, jnp.float32


def dot(a, b, dims):
    return lax.dot_general(a, b, (dims, ((), ())), preferred_element_type=F32)


def kernel(
    n, nt, lists, lin_q_h, lin_k_h, lin_v_h, att_q_h, att_k_h, att_v_h, gain_lin_h, gain_att_h,
    lin_out, att_out, inverse, lin_q, lin_k, lin_v, att_q, att_k, att_v, gain_lin, gain_att, wide_gains, kv, home, pre, first, scores,
    xout, xin, zout, zin, bout, bin_, pback, squares, sq_out, sq_in,
    lsem, kvs, kvr, hs_, hr, xs, xr, zs, zr, bs, br, ps, pr, ns, nr,
):
    ctx, tp = lax.axis_index("ctx"), lax.axis_index("tp")
    p, o = lax.rem(ctx, 2), lax.div(ctx, 2)
    core = lax.rem(tp, 2)
    chief, left = tp + 1 - core, tp - core
    lead = core == 1
    mate = ctx + 1 - 2 * p
    tokens = lin_q.shape[0]
    heads = lin_q.shape[1] // HD
    kv_heads = att_k.shape[1] // HD
    half = heads // 2
    has_prev, has_next = o > 0, o < n // 2 - 1
    side, ahead, behind = {"ctx": mate}, {"ctx": ctx + 2}, {"ctx": ctx - 2}

    other, mine = (1 - p) * half, p * half

    def columns(ref, h):
        return ref.at[:, pl.ds(pl.multiple_of(h * HD, HD), half * HD)]

    pairs = (
        (columns(lin_k_h, other), columns(lin_k, other)), (columns(lin_v_h, other), columns(lin_v, other)),
        (columns(lin_k_h, mine), columns(lin_k, mine)), (columns(lin_v_h, mine), columns(lin_v, mine)),
        (lin_q_h, lin_q),
        (gain_lin_h, gain_lin), (gain_att_h, gain_att),
        (att_q_h, att_q), (att_k_h, att_k), (att_v_h, att_v),
    )
    local = [pltpu.make_async_copy(s, d, lsem.at[i]) for i, (s, d) in enumerate(pairs)]
    barrier = pltpu.get_barrier_semaphore()

    def greet(where):
        pl.semaphore_signal(barrier, inc=1, device_id=where, device_id_type=MESH)

    greet({"ctx": mate, "tp": left})
    greet({"ctx": mate, "tp": chief})
    pl.when(has_prev)(lambda: greet(behind))
    pl.when(has_next)(lambda: greet(ahead))
    for k in range(1, nt):
        greet({"tp": lax.rem(tp + k, nt)})
    for c in local:
        c.start()

    def remote(src, dst, ssem, rsem, where):
        return pltpu.make_async_remote_copy(
            src_ref=src, dst_ref=dst, send_sem=ssem, recv_sem=rsem,
            device_id=where, device_id_type=MESH,
        )

    pieces = [(0, 0, 0, tokens), (0, 1, 0, tokens), (1, 0, 0, tokens), (1, 1, 0, tokens // 2), (1, 1, tokens // 2, tokens // 2)]

    def kv_copies(src, slot, sem, where):
        return [
            remote(
                src[a].at[pl.ds(r, m), pl.ds(g * HD, HD)], kv.at[slot, a, pl.ds(r, m), pl.ds(g * HD, HD)],
                kvs.at[sem, i], kvr.at[sem, i], where,
            )
            for i, (g, a, r, m) in enumerate(pieces)
        ]

    kv_src = (att_k_h, att_v_h)
    kv_ahead = kv_copies(kv_src, 1, 1, ahead)
    kv_side = kv_copies(kv_src, 0, 0, side)
    kv_pass = kv_copies((kv.at[1, 0], kv.at[1, 1]), 0, 0, side)
    which = range(len(pieces))

    def send_ahead(ids):
        for i in ids:
            pl.when(has_next)(kv_ahead[i].start)

    def send_side(ids):
        for i in ids:
            pl.when(p == 0)(kv_side[i].start)

    def lanes(h):
        return pl.ds(pl.multiple_of(h * HD, HD), HD)

    x_copy = [
        remote(xout.at[j], xin.at[core, j], xs.at[j], xr.at[core, j], {"ctx": mate, "tp": chief})
        for j in range(half)
    ]
    x_recv = [
        [remote(xout.at[j], xin.at[c, j], xs.at[j], xr.at[c, j], side) for j in range(half)]
        for c in range(2)
    ]
    h_copy = [
        remote(home.at[0, j], home.at[0, j], hs_.at[j], hr.at[j], {"tp": chief})
        for j in range(half)
    ]
    z_copy = [
        [remote(zout.at[c, j], zin.at[c, j], zs.at[c, j], zr.at[c, j], ahead) for j in range(half)]
        for c in range(2)
    ]
    b_copy = [
        [
            remote(bout.at[c, j], bin_.at[j], bs.at[c, j], br.at[j], {"ctx": mate, "tp": left + c})
            for j in range(half)
        ]
        for c in range(2)
    ]
    p_copy = [
        remote(pback.at[j], pre.at[j], ps.at[j], pr.at[j], {"tp": left}) for j in range(half)
    ]
    local[0].wait()
    local[1].wait()
    for j in range(half):
        h = other + j
        xout[j] = dot(lin_k[:, lanes(h)], lin_v[:, lanes(h)], ((0,), (0,))).astype(BF16)
    @pl.when(jnp.logical_not(has_prev))
    def _():
        kv[1] = jnp.zeros_like(kv[1])

        @pl.when(p == 0)
        def _():
            kv[0] = jnp.zeros_like(kv[0])
            bin_[...] = jnp.zeros_like(bin_)

    pl.semaphore_wait(barrier, nt + 1 + has_prev.astype(jnp.int32) + has_next.astype(jnp.int32))

    send_x = (p == 0) | has_next
    take_x = (p == 1) | has_next
    send_b = (p == 0) | has_prev
    take_b = (p == 1) | has_prev

    def start_x(first_head=0, end=half):
        for j in range(first_head, end):
            x_copy[j].start()

    rest = which[2:]
    yields = lead & (o < 2)
    pl.when(send_x & (o < 2))(lambda: start_x(0, half // 2))
    pl.when(send_x & (o < 2) & jnp.logical_not(lead))(lambda: start_x(half // 2))
    send_ahead((0,))
    send_ahead((1,))
    pl.when(jnp.logical_not(yields))(lambda: send_side((0, 1)))
    pl.when((o > 0) | jnp.logical_not(lead))(lambda: send_ahead((2,)))
    pl.when((o > 1) | (o == 1) & (jnp.logical_not(lead) | (p == 1)))(lambda: send_ahead((3, 4)))
    pl.when(send_x & (o >= 2) & has_next)(start_x)
    pl.when(jnp.logical_not(yields))(lambda: send_side(rest))
    pl.when(send_x & (o >= 2) & jnp.logical_not(has_next))(start_x)

    local[2].wait()
    local[3].wait()
    for j in range(half):
        h = mine + j
        home[core, j] = dot(lin_k[:, lanes(h)], lin_v[:, lanes(h)], ((0,), (0,)))

    @pl.when(jnp.logical_not(lead))
    def _():
        for j in range(half):
            h_copy[j].start()

    @pl.when(yields)
    def _():
        pl.when(send_x)(lambda: start_x(half // 2))
        send_side(which)


    for c in local[4:7]:
        c.wait()
    wide_gains[0] = gain_lin[...].astype(F32)
    wide_gains[1] = gain_att[...].astype(F32)
    row = lax.broadcasted_iota(jnp.int32, (BLK, BLK), 0)
    col = lax.broadcasted_iota(jnp.int32, (BLK, BLK), 1)
    lower = row >= col
    blocks = tokens // BLK
    for h in range(heads):
        hs = pl.ds(h * HD, HD)
        for b in range(blocks):
            rows = pl.ds(b * BLK, BLK)
            s = dot(lin_q[rows, hs], lin_k[rows, hs], ((1,), (1,)))
            scores[rows, hs] = jnp.where(lower, s, 0.0).astype(BF16)
        first[h] = dot(lin_k[0:BLK, hs], lin_v[0:BLK, hs], ((0,), (0,)))

    def forward(ids):
        @pl.when(has_prev)
        def _():
            for i in ids:
                kv_ahead[i].wait_recv()
                pl.when(p == 1)(kv_pass[i].start)

    def finish(h, prefix, fresh):
        for b in range(blocks):
            rows = pl.ds(b * BLK, BLK)
            low = (prefix if b == 0 else prefix + first[h]).astype(BF16)
            lhs = jnp.concatenate([scores[rows, lanes(h)], lin_q[rows, lanes(h)]], axis=1)
            rhs = jnp.concatenate([lin_v[rows, lanes(h)], low], axis=0)
            r = dot(lhs, rhs, ((1,), (0,)))
            lin_out[rows, lanes(h)] = r * wide_gains[0, pl.ds(h, 1)]
            squares[0, rows] = r * r if fresh else squares[0, rows] + r * r

    def link(c, j):
        @pl.when(has_prev)
        def _():
            z_copy[c][j].wait_recv()

        @pl.when(jnp.logical_not(has_prev))
        def _():
            zin[c, j] = jnp.zeros_like(zin[c, j])

        if c == 0:
            h_copy[j].wait_recv()
        before, here = zin[c, j].astype(F32), home[c, j]
        @pl.when(has_next)
        def _():
            x_recv[c][j].wait_recv()
            zout[c, j] = (before + here + xin[c, j].astype(F32)).astype(BF16)
            z_copy[c][j].start()
        bout[c, j] = jnp.where(p == 0, before + here, before).astype(BF16)
        pl.when(send_b)(b_copy[c][j].start)
        back = pback if c == 0 else pre

        @pl.when(p == 0)
        def _():
            back[j] = before

        @pl.when(p == 1)
        def _():
            pl.when(jnp.logical_not(has_next))(x_recv[c][j].wait_recv)
            back[j] = before + xin[c, j].astype(F32)

        if c == 0:
            p_copy[j].start()
        else:
            finish(mine + j, pre[j], j == 0)

    quarter = half // 2
    steps = [(1, j) for j in range(quarter)] + [(0, j) for j in range(half)] + [(1, j) for j in range(quarter, half)]

    def chain():
        for c, j in steps:
            link(c, j)

    def weave(at=()):
        for k, (c, j) in enumerate(steps):
            forward([i for i, step in at if step == k])
            link(c, j)

    inner = lead & has_prev & has_next
    final = lead & has_prev & jnp.logical_not(has_next)
    woven = inner & (o >= 2) & (p == 1)

    @pl.when(lead & jnp.logical_not(has_prev))
    def _():
        chain()
        send_ahead((2, 3, 4))

    def late_kv():
        for j in range(half):
            p_copy[j].wait_recv()
        send_ahead((3, 4))

    for c in local[7:]:
        c.wait()
    factor = (HD ** -0.5) * math.log2(math.e)
    bias = []
    for b in range(blocks):
        parts = []
        for i in range(SPAN - 1):
            key_block = ctx * blocks + b - (SPAN - 1) + i
            hit = lists[b, 0] == key_block
            for e in range(1, 4):
                hit = hit | (lists[b, e] == key_block)
            value = jnp.where(hit & (key_block >= 0), 0.0, NEG).astype(F32)
            parts.append(jnp.full((1, BLK), value, F32))
        bias.append(parts)

    kept, weights, scales = {}, {}, {}

    def group_of(g):
        return range(g * heads // kv_heads, (g + 1) * heads // kv_heads)

    def queries_of(g, b):
        rows = pl.ds(b * BLK, BLK)
        return jnp.concatenate([att_q[rows, pl.ds(h * HD, HD)] for h in group_of(g)], axis=0)

    def window(g, b, a, own):
        gs = pl.ds(g * HD, HD)
        return jnp.concatenate([kv[1, a, b * BLK:, gs], own[: (b + 1) * BLK, gs]], axis=0)

    def weigh_near(g):
        for b in range(blocks):
            keys = window(g, b, 0, att_k)
            sall = dot(queries_of(g, b), keys, ((1,), (1,)))
            cut = sall.shape[1] - BLK
            add = jnp.concatenate(bias[b][: blocks - b] + bias[b][2 * blocks - b:], axis=1)
            wall = []
            for i in range(len(group_of(g))):
                s = sall[i * BLK:(i + 1) * BLK]
                s = jnp.concatenate([s[:, :cut] + add, jnp.where(lower, s[:, cut:], NEG)], axis=1)
                m = jnp.max(s, axis=1, keepdims=True)
                e = jnp.exp2((s - m) * factor)
                kept[g, b, i] = (m, jnp.sum(e, axis=1, keepdims=True))
                wall.append(e.astype(BF16))
            weights[g, b] = jnp.concatenate(wall, axis=0)

    def sum_near(g):
        for b in range(blocks):
            rows = pl.ds(b * BLK, BLK)
            rall = dot(weights.pop((g, b)), window(g, b, 1, att_v), ((1,), (0,)))
            for i, h in enumerate(group_of(g)):
                att_out[rows, pl.ds(h * HD, HD)] = rall[i * BLK:(i + 1) * BLK]

    def await_far(g, which_of):
        for i in which:
            if pieces[i][:2] == (g, which_of):
                pl.when((p == 1) | has_prev)(kv_side[i].wait_recv)

    def weigh_far(g):
        gs = pl.ds(g * HD, HD)
        await_far(g, 0)
        for b in range(blocks):
            sall = dot(queries_of(g, b), kv[0, 0, :, gs], ((1,), (1,)))
            add = jnp.concatenate(bias[b][blocks - b: 2 * blocks - b], axis=1)
            wall, scale = [], []
            scales[g, b] = scale
            for i in range(len(group_of(g))):
                m_near, l_near = kept[g, b, i]
                s = sall[i * BLK:(i + 1) * BLK] + add
                m = jnp.maximum(m_near, jnp.max(s, axis=1, keepdims=True))
                e = jnp.exp2((s - m) * factor)
                keep = jnp.exp2((m_near - m) * factor)
                inv = 1.0 / (keep * l_near + jnp.sum(e, axis=1, keepdims=True))
                scale.append((keep * inv, inv))
                wall.append(e.astype(BF16))
            weights[g, b] = jnp.concatenate(wall, axis=0)

    def sum_far(g):
        gs = pl.ds(g * HD, HD)
        await_far(g, 1)
        for b in range(blocks):
            rows, scale = pl.ds(b * BLK, BLK), scales[g, b]
            rall = dot(weights[g, b], kv[0, 1, :, gs], ((1,), (0,)))
            sq = None if g == 0 else squares[1, rows]
            for i, h in enumerate(group_of(g)):
                hs = pl.ds(h * HD, HD)
                r = att_out[rows, hs] * scale[i][0] + rall[i * BLK:(i + 1) * BLK] * scale[i][1]
                att_out[rows, hs] = r * wide_gains[1, h:h + 1]
                sq = r * r if sq is None else sq + r * r
            squares[1, rows] = sq

    def finish_mine():
        for j in range(half):
            pl.when(o > 0)(p_copy[j].wait_recv)
            finish(mine + j, pre[j], j == 0)

    def far_first():
        weigh_far(0)
        sum_far(0)

    def finish_other():
        for j in range(half):
            pl.when(take_b)(b_copy[0][j].wait_recv)
            finish(other + j, bin_[j].astype(F32), False)

    deep = inner & (o >= 2)
    far_soon = (o >= 2) & (p == 1) & lead
    forward((0,))
    weigh_near(0)
    forward((1,))
    sum_near(0)
    pl.when(inner & (o < 2))(weave)
    pl.when(inner & (o == 1) & (p == 0))(lambda: send_ahead((3, 4)))
    pl.when(far_soon)(far_first)
    pl.when(jnp.logical_not(lead) & (o == 0))(late_kv)
    pl.when(jnp.logical_not(lead) & (o == 0))(finish_mine)
    forward((2,))
    weigh_near(1)
    pl.when(woven)(lambda: weave(((3, 2), (4, 4))))
    pl.when(deep & (p == 0))(weave)
    pl.when(jnp.logical_not(far_soon))(far_first)
    pl.when(jnp.logical_not(woven))(lambda: forward((3, 4)))
    sum_near(1)
    pl.when(final & (p == 0))(chain)
    weigh_far(1)
    pl.when(final & (p == 1))(chain)
    pl.when(jnp.logical_not(lead) & (o > 0))(finish_mine)
    pl.when(has_next)(finish_other)
    sum_far(1)
    pl.when(jnp.logical_not(has_next))(finish_other)

    def as_row(sq):
        return jnp.sum(sq.T, axis=0, keepdims=True)

    top = lax.broadcasted_iota(jnp.int32, (8, tokens), 0) == 0
    sums = jnp.where(top, as_row(squares[0]), as_row(squares[1]))
    sq_out[...] = sums
    n_copy = [
        remote(sq_out, sq_in.at[k - 1], ns.at[k - 1], nr.at[k - 1], {"tp": lax.rem(tp + k, nt)})
        for k in range(1, nt)
    ]
    for c in n_copy:
        c.start()
    for i in which:
        pl.when(has_next)(kv_ahead[i].wait_send)
        pl.when(p == 0)(kv_side[i].wait_send)

    @pl.when((p == 1) & has_prev)
    def _():
        for i in which:
            kv_pass[i].wait_send()

    for j in range(half):
        pl.when(send_x)(x_copy[j].wait_send)
        pl.when(jnp.logical_not(lead))(h_copy[j].wait_send)

    @pl.when(lead)
    def _():
        for c in range(2):
            for j in range(half):
                pl.when(has_next)(z_copy[c][j].wait_send)
                pl.when(send_b)(b_copy[c][j].wait_send)
        for j in range(half):
            p_copy[j].wait_send()

    for k in range(nt - 1):
        n_copy[k].wait_recv()
        sums = sums + sq_in[k]
    inverse[...] = lax.rsqrt(sums * (1.0 / (nt * heads * HD)) + EPS)
    for c in n_copy:
        c.wait_send()


def combine(inverse, lin_out, att_out, out_h, out, sem):
    tokens, width = out.shape

    def as_column(r):
        return jnp.broadcast_to(r, (HD, tokens)).T

    lin_inv, att_inv = as_column(inverse[0:1]), as_column(inverse[1:2])
    cuts = 4
    copies = []
    for q in range(cuts):
        m = tokens // cuts
        rows = pl.ds(q * m, m)
        li, ai = lin_inv[q * m:(q + 1) * m], att_inv[q * m:(q + 1) * m]
        for h in range(width // HD):
            hs = pl.ds(h * HD, HD)
            out[rows, hs] = (lin_out[rows, hs] * li + att_out[rows, hs] * ai).astype(BF16)
        copies.append(pltpu.make_async_copy(out.at[rows], out_h.at[rows], sem.at[q]))
        copies[-1].start()
    for c in copies:
        c.wait()


def per_device(n, nt, lin_q, lin_k, lin_v, att_q, att_k, att_v, block_lists, gain_lin, gain_att):
    tokens, columns = lin_q.shape
    heads, half = columns // HD, columns // HD // 2
    gain_lin, gain_att = gain_lin.reshape(heads, HD), gain_att.reshape(heads, HD)
    anywhere, inside = pl.BlockSpec(memory_space=pl.ANY), pl.BlockSpec(memory_space=pltpu.VMEM)
    wide, kv_wide = (tokens, columns), att_k.shape
    state, kv_heads = (half, HD, HD), kv_wide[1] // HD
    dma = pltpu.SemaphoreType.DMA
    lin_out, att_out, inverse = pl.pallas_call(
        functools.partial(kernel, n, nt),
        out_shape=(pltpu.VMEM(wide, F32), pltpu.VMEM(wide, F32), pltpu.VMEM((8, tokens), F32)),
        in_specs=[pl.BlockSpec(memory_space=pltpu.SMEM)] + [anywhere] * 8,
        out_specs=[inside] * 3,
        scratch_shapes=[
            pltpu.VMEM(wide, BF16), pltpu.VMEM(wide, BF16), pltpu.VMEM(wide, BF16),
            pltpu.VMEM(wide, BF16), pltpu.VMEM(kv_wide, BF16), pltpu.VMEM(kv_wide, BF16),
            pltpu.VMEM((heads, HD), BF16), pltpu.VMEM((heads, HD), BF16), pltpu.VMEM((2, heads, HD), F32),
            pltpu.VMEM((2, 2) + kv_wide, BF16),
            pltpu.VMEM((2,) + state, F32), pltpu.VMEM(state, F32), pltpu.VMEM((heads, HD, HD), F32),
            pltpu.VMEM(wide, BF16),
            pltpu.VMEM(state, BF16), pltpu.VMEM((2,) + state, BF16),
            pltpu.VMEM((2,) + state, BF16), pltpu.VMEM((2,) + state, BF16),
            pltpu.VMEM((2,) + state, BF16), pltpu.VMEM(state, BF16), pltpu.VMEM(state, F32),
            pltpu.VMEM((2, tokens, HD), F32),
            pltpu.VMEM((8, tokens), F32), pltpu.VMEM((nt - 1, 8, tokens), F32),
            dma((10,)), dma((2, 5)), dma((2, 5)),
            dma((half,)), dma((half,)),
            dma((half,)), dma((2, half)), dma((2, half)), dma((2, half)),
            dma((2, half)), dma((half,)), dma((half,)), dma((half,)),
            dma((nt - 1,)), dma((nt - 1,)),
        ],
        compiler_params=pltpu.CompilerParams(
            collective_id=0, has_side_effects=True, vmem_limit_bytes=62 * 2 ** 20 - 2 ** 17
        ),
    )(block_lists, lin_q, lin_k, lin_v, att_q, att_k, att_v, gain_lin, gain_att)
    return pl.pallas_call(
        combine,
        out_shape=jax.ShapeDtypeStruct(wide, BF16),
        in_specs=[inside] * 3,
        out_specs=anywhere,
        scratch_shapes=[pltpu.VMEM(wide, BF16), dma((4,))],
        compiler_params=pltpu.CompilerParams(vmem_limit_bytes=16 * 2 ** 20),
    )(inverse, lin_out, att_out)


def solution(mesh):
    wide = P("ctx", "tp")
    return jax.shard_map(
        functools.partial(per_device, mesh.shape["ctx"], mesh.shape["tp"]),
        mesh=mesh,
        in_specs=(wide,) * 6 + (P("ctx", None), P("tp"), P("tp")),
        out_specs=wide,
        check_vma=False,
    )
```

```python
import functools
import math

import jax
import jax.numpy as jnp
from jax import lax
from jax.experimental import pallas as pl
from jax.experimental.pallas import tpu as pltpu
from jax.sharding import PartitionSpec as P

HD = 128
BLK = 128
SPAN = 5
EPS = 1e-06
NEG = -1e30
MESH = pl.DeviceIdType.MESH
BF16, F32 = jnp.bfloat16, jnp.float32


def dot(a, b, dims):
    return lax.dot_general(a, b, (dims, ((), ())), preferred_element_type=F32)


def kernel(
    n, nt, lists, lin_q_h, lin_k_h, lin_v_h, att_q_h, att_k_h, att_v_h, gain_lin_h, gain_att_h,
    lin_out, att_out, inverse, lin_q, lin_k, lin_v, att_q, att_k, att_v, gain_lin, gain_att, wide_gains, kv, home, pre, first, scores,
    xout, xin, zout, zin, bout, bin_, pback, squares, sq_out, sq_in,
    lsem, kvs, kvr, hs_, hr, xs, xr, zs, zr, bs, br, ps, pr, ns, nr,
):
    ctx, tp = lax.axis_index("ctx"), lax.axis_index("tp")
    p, o = lax.rem(ctx, 2), lax.div(ctx, 2)
    core = lax.rem(tp, 2)
    chief, left = tp + 1 - core, tp - core
    lead = core == 1
    mate = ctx + 1 - 2 * p
    tokens = lin_q.shape[0]
    heads = lin_q.shape[1] // HD
    kv_heads = att_k.shape[1] // HD
    half = heads // 2
    has_prev, has_next = o > 0, o < n // 2 - 1
    side, ahead, behind = {"ctx": mate}, {"ctx": ctx + 2}, {"ctx": ctx - 2}

    other, mine = (1 - p) * half, p * half

    def columns(ref, h):
        return ref.at[:, pl.ds(pl.multiple_of(h * HD, HD), half * HD)]

    pairs = (
        (columns(lin_k_h, other), columns(lin_k, other)), (columns(lin_v_h, other), columns(lin_v, other)),
        (columns(lin_k_h, mine), columns(lin_k, mine)), (columns(lin_v_h, mine), columns(lin_v, mine)),
        (lin_q_h, lin_q),
        (gain_lin_h, gain_lin), (gain_att_h, gain_att),
        (att_q_h, att_q), (att_k_h, att_k), (att_v_h, att_v),
    )
    local = [pltpu.make_async_copy(s, d, lsem.at[i]) for i, (s, d) in enumerate(pairs)]
    barrier = pltpu.get_barrier_semaphore()

    def greet(where):
        pl.semaphore_signal(barrier, inc=1, device_id=where, device_id_type=MESH)

    greet({"ctx": mate, "tp": left})
    greet({"ctx": mate, "tp": chief})
    pl.when(has_prev)(lambda: greet(behind))
    pl.when(has_next)(lambda: greet(ahead))
    for k in range(1, nt):
        greet({"tp": lax.rem(tp + k, nt)})
    for c in local:
        c.start()

    def remote(src, dst, ssem, rsem, where):
        return pltpu.make_async_remote_copy(
            src_ref=src, dst_ref=dst, send_sem=ssem, recv_sem=rsem,
            device_id=where, device_id_type=MESH,
        )

    pieces = [(0, 0, 0, tokens), (0, 1, 0, tokens), (1, 0, 0, tokens), (1, 1, 0, tokens // 2), (1, 1, tokens // 2, tokens // 2)]

    def kv_copies(src, slot, sem, where):
        return [
            remote(
                src[a].at[pl.ds(r, m), pl.ds(g * HD, HD)], kv.at[slot, a, pl.ds(r, m), pl.ds(g * HD, HD)],
                kvs.at[sem, i], kvr.at[sem, i], where,
            )
            for i, (g, a, r, m) in enumerate(pieces)
        ]

    kv_src = (att_k_h, att_v_h)
    kv_ahead = kv_copies(kv_src, 1, 1, ahead)
    kv_side = kv_copies(kv_src, 0, 0, side)
    kv_pass = kv_copies((kv.at[1, 0], kv.at[1, 1]), 0, 0, side)
    which = range(len(pieces))

    def send_ahead(ids):
        for i in ids:
            pl.when(has_next)(kv_ahead[i].start)

    def send_side(ids):
        for i in ids:
            pl.when(p == 0)(kv_side[i].start)

    def lanes(h):
        return pl.ds(pl.multiple_of(h * HD, HD), HD)

    x_copy = [
        remote(xout.at[j], xin.at[core, j], xs.at[j], xr.at[core, j], {"ctx": mate, "tp": chief})
        for j in range(half)
    ]
    x_recv = [
        [remote(xout.at[j], xin.at[c, j], xs.at[j], xr.at[c, j], side) for j in range(half)]
        for c in range(2)
    ]
    h_copy = [
        remote(home.at[0, j], home.at[0, j], hs_.at[j], hr.at[j], {"tp": chief})
        for j in range(half)
    ]
    z_copy = [
        [remote(zout.at[c, j], zin.at[c, j], zs.at[c, j], zr.at[c, j], ahead) for j in range(half)]
        for c in range(2)
    ]
    b_copy = [
        [
            remote(bout.at[c, j], bin_.at[j], bs.at[c, j], br.at[j], {"ctx": mate, "tp": left + c})
            for j in range(half)
        ]
        for c in range(2)
    ]
    p_copy = [
        remote(pback.at[j], pre.at[j], ps.at[j], pr.at[j], {"tp": left}) for j in range(half)
    ]
    local[0].wait()
    local[1].wait()
    for j in range(half):
        h = other + j
        xout[j] = dot(lin_k[:, lanes(h)], lin_v[:, lanes(h)], ((0,), (0,))).astype(BF16)
    @pl.when(jnp.logical_not(has_prev))
    def _():
        kv[1] = jnp.zeros_like(kv[1])

        @pl.when(p == 0)
        def _():
            kv[0] = jnp.zeros_like(kv[0])
            bin_[...] = jnp.zeros_like(bin_)

    pl.semaphore_wait(barrier, nt + 1 + has_prev.astype(jnp.int32) + has_next.astype(jnp.int32))

    send_x = (p == 0) | has_next
    take_x = (p == 1) | has_next
    send_b = (p == 0) | has_prev
    take_b = (p == 1) | has_prev

    def start_x(first_head=0, end=half):
        for j in range(first_head, end):
            x_copy[j].start()

    rest = which[2:]
    yields = lead & (o < 2)
    pl.when(send_x & (o < 2))(lambda: start_x(0, half // 2))
    pl.when(send_x & (o < 2) & jnp.logical_not(lead))(lambda: start_x(half // 2))
    send_ahead((0,))
    send_ahead((1,))
    pl.when(jnp.logical_not(yields))(lambda: send_side((0, 1)))
    pl.when((o > 0) | jnp.logical_not(lead))(lambda: send_ahead((2,)))
    pl.when((o > 1) | (o == 1) & (jnp.logical_not(lead) | (p == 1)))(lambda: send_ahead((3, 4)))
    pl.when(send_x & (o >= 2) & has_next)(start_x)
    pl.when(jnp.logical_not(yields))(lambda: send_side(rest))
    pl.when(send_x & (o >= 2) & jnp.logical_not(has_next))(start_x)

    local[2].wait()
    local[3].wait()
    for j in range(half):
        h = mine + j
        home[core, j] = dot(lin_k[:, lanes(h)], lin_v[:, lanes(h)], ((0,), (0,)))

    @pl.when(jnp.logical_not(lead))
    def _():
        for j in range(half):
            h_copy[j].start()

    @pl.when(yields)
    def _():
        pl.when(send_x)(lambda: start_x(half // 2))
        send_side(which)


    for c in local[4:7]:
        c.wait()
    wide_gains[0] = gain_lin[...].astype(F32)
    wide_gains[1] = gain_att[...].astype(F32)
    row = lax.broadcasted_iota(jnp.int32, (BLK, BLK), 0)
    col = lax.broadcasted_iota(jnp.int32, (BLK, BLK), 1)
    lower = row >= col
    blocks = tokens // BLK
    for h in range(heads):
        hs = pl.ds(h * HD, HD)
        for b in range(blocks):
            rows = pl.ds(b * BLK, BLK)
            s = dot(lin_q[rows, hs], lin_k[rows, hs], ((1,), (1,)))
            scores[rows, hs] = jnp.where(lower, s, 0.0).astype(BF16)
        first[h] = dot(lin_k[0:BLK, hs], lin_v[0:BLK, hs], ((0,), (0,)))

    def forward(ids):
        @pl.when(has_prev)
        def _():
            for i in ids:
                kv_ahead[i].wait_recv()
                pl.when(p == 1)(kv_pass[i].start)

    def finish(h, prefix, fresh):
        for b in range(blocks):
            rows = pl.ds(b * BLK, BLK)
            low = (prefix if b == 0 else prefix + first[h]).astype(BF16)
            lhs = jnp.concatenate([scores[rows, lanes(h)], lin_q[rows, lanes(h)]], axis=1)
            rhs = jnp.concatenate([lin_v[rows, lanes(h)], low], axis=0)
            r = dot(lhs, rhs, ((1,), (0,)))
            lin_out[rows, lanes(h)] = r * wide_gains[0, pl.ds(h, 1)]
            squares[0, rows] = r * r if fresh else squares[0, rows] + r * r

    def link(c, j):
        @pl.when(has_prev)
        def _():
            z_copy[c][j].wait_recv()

        @pl.when(jnp.logical_not(has_prev))
        def _():
            zin[c, j] = jnp.zeros_like(zin[c, j])

        if c == 0:
            h_copy[j].wait_recv()
        before, here = zin[c, j].astype(F32), home[c, j]
        @pl.when(has_next)
        def _():
            x_recv[c][j].wait_recv()
            zout[c, j] = (before + here + xin[c, j].astype(F32)).astype(BF16)
            z_copy[c][j].start()
        bout[c, j] = jnp.where(p == 0, before + here, before).astype(BF16)
        pl.when(send_b)(b_copy[c][j].start)
        back = pback if c == 0 else pre

        @pl.when(p == 0)
        def _():
            back[j] = before

        @pl.when(p == 1)
        def _():
            pl.when(jnp.logical_not(has_next))(x_recv[c][j].wait_recv)
            back[j] = before + xin[c, j].astype(F32)

        if c == 0:
            p_copy[j].start()
        else:
            finish(mine + j, pre[j], j == 0)

    quarter = half // 2
    steps = [(1, j) for j in range(quarter)] + [(0, j) for j in range(half)] + [(1, j) for j in range(quarter, half)]

    def chain():
        for c, j in steps:
            link(c, j)

    def weave(at=()):
        for k, (c, j) in enumerate(steps):
            forward([i for i, step in at if step == k])
            link(c, j)

    inner = lead & has_prev & has_next
    final = lead & has_prev & jnp.logical_not(has_next)
    woven = inner & (o >= 2) & (p == 1)

    @pl.when(lead & jnp.logical_not(has_prev))
    def _():
        chain()
        send_ahead((2, 3, 4))

    def late_kv():
        for j in range(half):
            p_copy[j].wait_recv()
        send_ahead((3, 4))

    for c in local[7:]:
        c.wait()
    factor = (HD ** -0.5) * math.log2(math.e)
    bias = []
    for b in range(blocks):
        parts = []
        for i in range(SPAN - 1):
            key_block = ctx * blocks + b - (SPAN - 1) + i
            hit = lists[b, 0] == key_block
            for e in range(1, 4):
                hit = hit | (lists[b, e] == key_block)
            value = jnp.where(hit & (key_block >= 0), 0.0, NEG).astype(F32)
            parts.append(jnp.full((1, BLK), value, F32))
        bias.append(parts)

    kept, weights, scales = {}, {}, {}

    def group_of(g):
        return range(g * heads // kv_heads, (g + 1) * heads // kv_heads)

    def queries_of(g, b):
        rows = pl.ds(b * BLK, BLK)
        return jnp.concatenate([att_q[rows, pl.ds(h * HD, HD)] for h in group_of(g)], axis=0)

    def window(g, b, a, own):
        gs = pl.ds(g * HD, HD)
        return jnp.concatenate([kv[1, a, b * BLK:, gs], own[: (b + 1) * BLK, gs]], axis=0)

    def weigh_near(g):
        for b in range(blocks):
            keys = window(g, b, 0, att_k)
            sall = dot(queries_of(g, b), keys, ((1,), (1,)))
            cut = sall.shape[1] - BLK
            add = jnp.concatenate(bias[b][: blocks - b] + bias[b][2 * blocks - b:], axis=1)
            wall = []
            for i in range(len(group_of(g))):
                s = sall[i * BLK:(i + 1) * BLK]
                s = jnp.concatenate([s[:, :cut] + add, jnp.where(lower, s[:, cut:], NEG)], axis=1)
                m = jnp.max(s, axis=1, keepdims=True)
                e = jnp.exp2((s - m) * factor)
                kept[g, b, i] = (m, jnp.sum(e, axis=1, keepdims=True))
                wall.append(e.astype(BF16))
            weights[g, b] = jnp.concatenate(wall, axis=0)

    def sum_near(g):
        for b in range(blocks):
            rows = pl.ds(b * BLK, BLK)
            rall = dot(weights.pop((g, b)), window(g, b, 1, att_v), ((1,), (0,)))
            for i, h in enumerate(group_of(g)):
                att_out[rows, pl.ds(h * HD, HD)] = rall[i * BLK:(i + 1) * BLK]

    def await_far(g, which_of):
        for i in which:
            if pieces[i][:2] == (g, which_of):
                pl.when((p == 1) | has_prev)(kv_side[i].wait_recv)

    def weigh_far(g):
        gs = pl.ds(g * HD, HD)
        await_far(g, 0)
        for b in range(blocks):
            sall = dot(queries_of(g, b), kv[0, 0, :, gs], ((1,), (1,)))
            add = jnp.concatenate(bias[b][blocks - b: 2 * blocks - b], axis=1)
            wall, scale = [], []
            scales[g, b] = scale
            for i in range(len(group_of(g))):
                m_near, l_near = kept[g, b, i]
                s = sall[i * BLK:(i + 1) * BLK] + add
                m = jnp.maximum(m_near, jnp.max(s, axis=1, keepdims=True))
                e = jnp.exp2((s - m) * factor)
                keep = jnp.exp2((m_near - m) * factor)
                inv = 1.0 / (keep * l_near + jnp.sum(e, axis=1, keepdims=True))
                scale.append((keep * inv, inv))
                wall.append(e.astype(BF16))
            weights[g, b] = jnp.concatenate(wall, axis=0)

    def sum_far(g):
        gs = pl.ds(g * HD, HD)
        await_far(g, 1)
        for b in range(blocks):
            rows, scale = pl.ds(b * BLK, BLK), scales[g, b]
            rall = dot(weights[g, b], kv[0, 1, :, gs], ((1,), (0,)))
            sq = None if g == 0 else squares[1, rows]
            for i, h in enumerate(group_of(g)):
                hs = pl.ds(h * HD, HD)
                r = att_out[rows, hs] * scale[i][0] + rall[i * BLK:(i + 1) * BLK] * scale[i][1]
                att_out[rows, hs] = r * wide_gains[1, h:h + 1]
                sq = r * r if sq is None else sq + r * r
            squares[1, rows] = sq

    def finish_mine():
        for j in range(half):
            pl.when(o > 0)(p_copy[j].wait_recv)
            finish(mine + j, pre[j], j == 0)

    def far_first():
        weigh_far(0)
        sum_far(0)

    def finish_other():
        for j in range(half):
            pl.when(take_b)(b_copy[0][j].wait_recv)
            finish(other + j, bin_[j].astype(F32), False)

    deep = inner & (o >= 2)
    far_soon = (o >= 2) & (p == 1) & lead
    forward((0,))
    weigh_near(0)
    forward((1,))
    sum_near(0)
    pl.when(inner & (o < 2))(weave)
    pl.when(inner & (o == 1) & (p == 0))(lambda: send_ahead((3, 4)))
    pl.when(far_soon)(far_first)
    pl.when(jnp.logical_not(lead) & (o == 0))(late_kv)
    pl.when(jnp.logical_not(lead) & (o == 0))(finish_mine)
    forward((2,))
    weigh_near(1)
    pl.when(woven)(lambda: weave(((3, 5), (4, 7))))
    pl.when(deep & (p == 0))(weave)
    pl.when(jnp.logical_not(far_soon))(far_first)
    pl.when(jnp.logical_not(woven))(lambda: forward((3, 4)))
    sum_near(1)
    pl.when(final & (p == 0))(chain)
    weigh_far(1)
    pl.when(final & (p == 1))(chain)
    pl.when(jnp.logical_not(lead) & (o > 0))(finish_mine)
    pl.when(has_next)(finish_other)
    sum_far(1)
    pl.when(jnp.logical_not(has_next))(finish_other)

    def as_row(sq):
        return jnp.sum(sq.T, axis=0, keepdims=True)

    top = lax.broadcasted_iota(jnp.int32, (8, tokens), 0) == 0
    sums = jnp.where(top, as_row(squares[0]), as_row(squares[1]))
    sq_out[...] = sums
    n_copy = [
        remote(sq_out, sq_in.at[k - 1], ns.at[k - 1], nr.at[k - 1], {"tp": lax.rem(tp + k, nt)})
        for k in range(1, nt)
    ]
    for c in n_copy:
        c.start()
    for i in which:
        pl.when(has_next)(kv_ahead[i].wait_send)
        pl.when(p == 0)(kv_side[i].wait_send)

    @pl.when((p == 1) & has_prev)
    def _():
        for i in which:
            kv_pass[i].wait_send()

    for j in range(half):
        pl.when(send_x)(x_copy[j].wait_send)
        pl.when(jnp.logical_not(lead))(h_copy[j].wait_send)

    @pl.when(lead)
    def _():
        for c in range(2):
            for j in range(half):
                pl.when(has_next)(z_copy[c][j].wait_send)
                pl.when(send_b)(b_copy[c][j].wait_send)
        for j in range(half):
            p_copy[j].wait_send()

    for k in range(nt - 1):
        n_copy[k].wait_recv()
        sums = sums + sq_in[k]
    inverse[...] = lax.rsqrt(sums * (1.0 / (nt * heads * HD)) + EPS)
    for c in n_copy:
        c.wait_send()


def combine(inverse, lin_out, att_out, out_h, out, sem):
    tokens, width = out.shape

    def as_column(r):
        return jnp.broadcast_to(r, (HD, tokens)).T

    lin_inv, att_inv = as_column(inverse[0:1]), as_column(inverse[1:2])
    cuts = 4
    copies = []
    for q in range(cuts):
        m = tokens // cuts
        rows = pl.ds(q * m, m)
        li, ai = lin_inv[q * m:(q + 1) * m], att_inv[q * m:(q + 1) * m]
        for h in range(width // HD):
            hs = pl.ds(h * HD, HD)
            out[rows, hs] = (lin_out[rows, hs] * li + att_out[rows, hs] * ai).astype(BF16)
        copies.append(pltpu.make_async_copy(out.at[rows], out_h.at[rows], sem.at[q]))
        copies[-1].start()
    for c in copies:
        c.wait()


def per_device(n, nt, lin_q, lin_k, lin_v, att_q, att_k, att_v, block_lists, gain_lin, gain_att):
    tokens, columns = lin_q.shape
    heads, half = columns // HD, columns // HD // 2
    gain_lin, gain_att = gain_lin.reshape(heads, HD), gain_att.reshape(heads, HD)
    anywhere, inside = pl.BlockSpec(memory_space=pl.ANY), pl.BlockSpec(memory_space=pltpu.VMEM)
    wide, kv_wide = (tokens, columns), att_k.shape
    state, kv_heads = (half, HD, HD), kv_wide[1] // HD
    dma = pltpu.SemaphoreType.DMA
    lin_out, att_out, inverse = pl.pallas_call(
        functools.partial(kernel, n, nt),
        out_shape=(pltpu.VMEM(wide, F32), pltpu.VMEM(wide, F32), pltpu.VMEM((8, tokens), F32)),
        in_specs=[pl.BlockSpec(memory_space=pltpu.SMEM)] + [anywhere] * 8,
        out_specs=[inside] * 3,
        scratch_shapes=[
            pltpu.VMEM(wide, BF16), pltpu.VMEM(wide, BF16), pltpu.VMEM(wide, BF16),
            pltpu.VMEM(wide, BF16), pltpu.VMEM(kv_wide, BF16), pltpu.VMEM(kv_wide, BF16),
            pltpu.VMEM((heads, HD), BF16), pltpu.VMEM((heads, HD), BF16), pltpu.VMEM((2, heads, HD), F32),
            pltpu.VMEM((2, 2) + kv_wide, BF16),
            pltpu.VMEM((2,) + state, F32), pltpu.VMEM(state, F32), pltpu.VMEM((heads, HD, HD), F32),
            pltpu.VMEM(wide, BF16),
            pltpu.VMEM(state, BF16), pltpu.VMEM((2,) + state, BF16),
            pltpu.VMEM((2,) + state, BF16), pltpu.VMEM((2,) + state, BF16),
            pltpu.VMEM((2,) + state, BF16), pltpu.VMEM(state, BF16), pltpu.VMEM(state, F32),
            pltpu.VMEM((2, tokens, HD), F32),
            pltpu.VMEM((8, tokens), F32), pltpu.VMEM((nt - 1, 8, tokens), F32),
            dma((10,)), dma((2, 5)), dma((2, 5)),
            dma((half,)), dma((half,)),
            dma((half,)), dma((2, half)), dma((2, half)), dma((2, half)),
            dma((2, half)), dma((half,)), dma((half,)), dma((half,)),
            dma((nt - 1,)), dma((nt - 1,)),
        ],
        compiler_params=pltpu.CompilerParams(
            collective_id=0, has_side_effects=True, vmem_limit_bytes=62 * 2 ** 20 - 2 ** 17
        ),
    )(block_lists, lin_q, lin_k, lin_v, att_q, att_k, att_v, gain_lin, gain_att)
    return pl.pallas_call(
        combine,
        out_shape=jax.ShapeDtypeStruct(wide, BF16),
        in_specs=[inside] * 3,
        out_specs=anywhere,
        scratch_shapes=[pltpu.VMEM(wide, BF16), dma((4,))],
        compiler_params=pltpu.CompilerParams(vmem_limit_bytes=16 * 2 ** 20),
    )(inverse, lin_out, att_out)


def solution(mesh):
    wide = P("ctx", "tp")
    return jax.shard_map(
        functools.partial(per_device, mesh.shape["ctx"], mesh.shape["tp"]),
        mesh=mesh,
        in_specs=(wide,) * 6 + (P("ctx", None), P("tp"), P("tp")),
        out_specs=wide,
        check_vma=False,
    )
```
